32 devices in a mesh: seq: 4 (over z), dp: 8 (over y, x, core).
Axes of the slice: x: 2, y: 2, z: 4, core: 2. Of those that a mesh axis runs over, the one named last changes fastest.
Arguments:
- stream: float32 [8, 512, 1152], P('dp', 'seq'), may hold values from -50 to 50
- stream_grad: float32 [8, 512, 1152], P('dp', 'seq'), may hold values from -6 to 6
- lengths: int32 [8, 4], P('dp'), may hold values from 1 to 384, 512 in all within a row
- w_qkv: bfloat16 [1152, 1536], P(('seq', 'dp')), may hold values from -0.1875 to 0.1875
- w_out: bfloat16 [1024, 1152], P(('seq', 'dp')), may hold values from -0.1875 to 0.1875
- w_gate: bfloat16 [6912, 1152], P(('seq', 'dp')), may hold values from -0.1875 to 0.1875
- w_up: bfloat16 [6912, 1152], P(('seq', 'dp')), may hold values from -0.1875 to 0.1875
- w_down: bfloat16 [6912, 1152], P(('seq', 'dp')), may hold values from -0.078125 to 0.078125
- g_attn_in: float32 [1152], replicated, may hold values from 0.25 to 1.75
- g_query: float32 [256], replicated, may hold values from 0.25 to 1.75
- g_key: float32 [256], replicated, may hold values from 0.25 to 1.75
- g_attn_out: float32 [1152], replicated, may hold values from 0.25 to 1.75
- g_ffn_in: float32 [1152], replicated, may hold values from 0.25 to 1.75
- g_ffn_out: float32 [1152], replicated, may hold values from 0.25 to 1.75
Outputs:
- result: float32 [8, 512, 1152], P('dp', 'seq')
- input_grad: float32 [8, 512, 1152], P('dp', 'seq')
- grad_w_qkv: float32 [1152, 1536], P(('seq', 'dp'))
- grad_w_out: float32 [1024, 1152], P(('seq', 'dp'))
- grad_w_gate: float32 [6912, 1152], P(('seq', 'dp'))
- grad_w_up: float32 [6912, 1152], P(('seq', 'dp'))
- grad_w_down: float32 [6912, 1152], P(('seq', 'dp'))
- grad_g_attn_in: float32 [1152], P(('seq', 'dp'))
- grad_g_query: float32 [256], P(('seq', 'dp'))
- grad_g_key: float32 [256], P(('seq', 'dp'))
- grad_g_attn_out: float32 [1152], P(('seq', 'dp'))
- grad_g_ffn_in: float32 [1152], P(('seq', 'dp'))
- grad_g_ffn_out: float32 [1152], P(('seq', 'dp'))
The draws below stay inside these ranges and needn't reach their ends.
Inputs may be any that keep to these rules, and one draw needn't show every extreme that they name: Each row lists the lengths of the 4 sequences packed in order into one group; they sum to 512.
All inputs are finite; a program needn't handle non-finite values.
Results may differ from the reference program's by a relative error of at most 0.015.
Values may be sent and summed in bfloat16 or wider, within the bound.
A program may use at most 128 MiB of HBM per device.

```python
import math
import jax
import jax.numpy as jnp
import numpy as np
from jax import lax

D = 1152
HEADS = 4
HEAD_DIM = 256
FF = 6912
WINDOW = 512
SEQS = 4
SEQ_TOKENS = 512
GROUPS = 8
QUERY_WIDTH = 1024
QKV_WIDTH = 1536


def draw_stream(key, part):
    first, second, third = jax.random.split(key, 3)
    shape = (GROUPS, SEQ_TOKENS, D)
    base = jax.random.truncated_normal(first, -5.0, 5.0, shape, jnp.float32)
    row_scale = jnp.exp(jax.random.uniform(second, (GROUPS, SEQ_TOKENS, 1), jnp.float32, -1.15, 1.15))
    col_scale = jnp.exp(jax.random.uniform(third, (1, 1, D), jnp.float32, -1.15, 1.15))
    return base * row_scale * col_scale


def shard_levels(rng, dims, cuts, smallest, largest):
    level, own = 1.0, jax.random.fold_in(rng, 6)
    for axis_at, shards_of in cuts:
        heights = jnp.exp(jax.random.uniform(jax.random.fold_in(own, axis_at), (shards_of,), jnp.float32, smallest / len(cuts), largest / len(cuts)))
        level = level * jnp.repeat(heights, dims[axis_at] // shards_of).reshape([-1 if axis == axis_at else 1 for axis in range(len(dims))])
    return level


def length_profile(number_of, total, most, slope):
    loads = [(1 << 20) // math.isqrt(standing ** slope) + 1 for standing in range(2, number_of + 1)]
    rest, given = total - most - (number_of - 1), [1] * (number_of - 1)
    while rest > 0:
        movable = [i for i in range(number_of - 1) if given[i] < most]
        mass, budget = sum([loads[i] for i in movable]), rest
        for i in movable:
            extra = min(most - given[i], max(1, budget * loads[i] // mass), rest)
            given[i] = given[i] + extra
            rest = rest - extra
    return np.array([most] + given)


def ragged_sizes(key, number_of, total, most, slope):
    if number_of == 2:
        one = jax.random.randint(key, (), max(1, total - most), min(most, total - 1) + 1)
        return jnp.stack([one, total - one])
    sizes = jnp.asarray(length_profile(number_of, total, most, slope), jnp.int32)
    couples = (number_of - 1) // 2
    donor, sink = sizes[1:1 + 2 * couples:2], sizes[2:2 + 2 * couples:2]
    room = jnp.minimum(donor - 1, most - sink)
    passed = jax.random.randint(jax.random.fold_in(key, 1), (couples,), 0, 1 << 20) % (room + 1)
    sizes = sizes.at[1:1 + 2 * couples:2].set(donor - passed).at[2:2 + 2 * couples:2].set(sink + passed)
    return sizes[jax.random.permutation(jax.random.fold_in(key, 2), number_of)]


def gaussian(rng, extent, width, reach, cuts=(), kind=jnp.bfloat16):
    factor_of = shard_levels(rng, extent, cuts, -0.22, 0.18) if cuts else 1.0
    values = jax.random.normal(rng, extent, jnp.float32) * width * factor_of
    return jnp.minimum(jnp.maximum(values, -reach), reach).astype(kind)


def setup_inputs(seed: int = 0) -> dict:
    streams_of = jax.random.split(jax.random.key(seed), 15)
    stream = draw_stream(jax.random.fold_in(streams_of[14], 71), 0)
    stream_grad = gaussian(streams_of[1], (GROUPS, SEQ_TOKENS, D), 1.0, 6.0, ((0, 8), (1, 4)), jnp.float32)
    lengths = jax.vmap(lambda own: ragged_sizes(own, SEQS, SEQ_TOKENS, SEQ_TOKENS * 3 // 4, 2))(jax.random.split(streams_of[2], GROUPS)).reshape((GROUPS, SEQS)).astype(jnp.int32)
    w_qkv = gaussian(streams_of[3], (D, QKV_WIDTH), D ** -0.5, 0.1875, ((0, 32),))
    w_out = gaussian(streams_of[4], (QUERY_WIDTH, D), QUERY_WIDTH ** -0.5, 0.1875, ((0, 32),))
    w_gate = gaussian(streams_of[5], (FF, D), D ** -0.5, 0.1875, ((0, 32),))
    w_up = gaussian(streams_of[6], (FF, D), D ** -0.5, 0.1875, ((0, 32),))
    w_down = gaussian(streams_of[7], (FF, D), FF ** -0.5, 0.078125, ((0, 32),))
    g_attn_in = jnp.clip(1.0 + 0.15 * jax.random.normal(streams_of[8], (D,), jnp.float32), 0.25, 1.75)
    g_query = jnp.clip(1.0 + 0.15 * jax.random.normal(streams_of[9], (HEAD_DIM,), jnp.float32), 0.25, 1.75)
    g_key = jnp.clip(1.0 + 0.15 * jax.random.normal(streams_of[10], (HEAD_DIM,), jnp.float32), 0.25, 1.75)
    g_attn_out = jnp.clip(1.0 + 0.15 * jax.random.normal(streams_of[11], (D,), jnp.float32), 0.25, 1.75)
    g_ffn_in = jnp.clip(1.0 + 0.15 * jax.random.normal(streams_of[12], (D,), jnp.float32), 0.25, 1.75)
    g_ffn_out = jnp.clip(1.0 + 0.15 * jax.random.normal(streams_of[13], (D,), jnp.float32), 0.25, 1.75)
    return {"stream": stream, "stream_grad": stream_grad, "lengths": lengths, "w_qkv": w_qkv, "w_out": w_out, "w_gate": w_gate, "w_up": w_up, "w_down": w_down, "g_attn_in": g_attn_in, "g_query": g_query, "g_key": g_key, "g_attn_out": g_attn_out, "g_ffn_in": g_ffn_in, "g_ffn_out": g_ffn_out}


EPSILON = 1e-06
GELU_SLOPE = math.sqrt(2.0 / math.pi)
GELU_CUBIC = 0.044715

def inv_root(vector):
    return lax.rsqrt(lax.optimization_barrier(jnp.mean(vector * vector, axis=-1, keepdims=True)) + EPSILON)

def norm_back(grad, unit_part, root_part, gain):
    scaled = grad * gain
    return root_part * (scaled - unit_part * lax.optimization_barrier(jnp.mean(scaled * unit_part, axis=-1, keepdims=True)))

def gelu_pair(gate):
    inner = jnp.tanh(GELU_SLOPE * (gate + GELU_CUBIC * gate * gate * gate))
    gelu_value = 0.5 * gate * (1.0 + inner)
    gelu_slope = 0.5 * (1.0 + inner) + 0.5 * gate * (1.0 - inner * inner) * GELU_SLOPE * (1.0 + 3.0 * GELU_CUBIC * gate * gate)
    return (gelu_value, gelu_slope)

def turn_half(vector):
    half = vector.shape[-1] // 2
    return jnp.concatenate([-vector[..., half:], vector[..., :half]], axis=-1)

def seq_begin(index, starts):
    return lax.optimization_barrier(jnp.max(jnp.where(starts[None, :] <= index[:, None], starts[None, :], 0), axis=1)).astype(jnp.int32)

def rope_tables(position, head):
    freq = jnp.exp(-math.log(10000.0) * jnp.arange(head // 2, dtype=jnp.float32) * (2.0 / head))
    angle = position[:, None] * freq[None, :]
    angle = jnp.concatenate([angle, angle], axis=1)
    return (jnp.cos(angle), jnp.sin(angle))

def dot32(left, right):
    return jnp.dot(left, right, preferred_element_type=jnp.float32)

def group_pass(rows_in, rows_grad, lens, w_qkv, w_out, w_gate, w_up, w_down, g_attn_in, g_query, g_key, g_attn_out, g_ffn_in, g_ffn_out):
    count = rows_in.shape[0]
    qwidth = HEADS * HEAD_DIM
    index = jnp.arange(count, dtype=jnp.int32)
    starts = (jnp.cumsum(lens) - lens).astype(jnp.int32)
    begin = seq_begin(index, starts)
    cos_t, sin_t = rope_tables((index - begin).astype(jnp.float32), HEAD_DIM)
    mask = (begin[:, None] == begin[None, :]) & (index[None, :] <= index[:, None]) & (index[:, None] - index[None, :] < WINDOW)
    full_mask = mask[:, None, :]
    scale = 1.0 / math.sqrt(HEAD_DIM)
    root_attn = inv_root(rows_in)
    unit_attn = rows_in * root_attn
    attn_input = (unit_attn * g_attn_in).astype(jnp.bfloat16)
    projected = dot32(attn_input, w_qkv)
    query = projected[:, :qwidth].reshape(count, HEADS, HEAD_DIM)
    key_raw = projected[:, qwidth:qwidth + HEAD_DIM]
    value_raw = projected[:, qwidth + HEAD_DIM:]
    root_query = inv_root(query)
    unit_query = query * root_query
    query_norm = unit_query * g_query
    root_key = inv_root(key_raw)
    unit_key = key_raw * root_key
    key_norm = unit_key * g_key
    query_rot = query_norm * cos_t[:, None, :] + turn_half(query_norm) * sin_t[:, None, :]
    key_rot = key_norm * cos_t + turn_half(key_norm) * sin_t
    query_b = query_rot.astype(jnp.bfloat16)
    key_b = key_rot.astype(jnp.bfloat16)
    value_b = value_raw.astype(jnp.bfloat16)
    scores = jnp.einsum('qhd,kd->qhk', query_b.astype(jnp.float32), key_b.astype(jnp.float32)) * scale
    logsum = jnp.log(lax.optimization_barrier(jnp.sum(jnp.where(full_mask, jnp.exp(scores), 0.0), axis=-1)))
    probs = jnp.where(full_mask, jnp.exp(scores - logsum[..., None]), 0.0)
    probs_b = probs.astype(jnp.bfloat16)
    mixed = jnp.einsum('qhk,kd->qhd', probs_b.astype(jnp.float32), value_b.astype(jnp.float32))
    mixed_b = mixed.reshape(count, qwidth).astype(jnp.bfloat16)
    attn_out = dot32(mixed_b, w_out)
    root_post = inv_root(attn_out)
    unit_post = attn_out * root_post
    hidden_in = rows_in + unit_post * g_attn_out
    root_ffn = inv_root(hidden_in)
    unit_ffn = hidden_in * root_ffn
    ffn_input = (unit_ffn * g_ffn_in).astype(jnp.bfloat16)
    gate = dot32(ffn_input, w_gate.T)
    up_part = dot32(ffn_input, w_up.T)
    gelu_value, gelu_slope = gelu_pair(gate)
    hidden = (gelu_value * up_part).astype(jnp.bfloat16)
    ffn_out = dot32(hidden, w_down)
    root_out = inv_root(ffn_out)
    unit_out = ffn_out * root_out
    result = hidden_in + unit_out * g_ffn_out
    grad_g_ffn_out = lax.optimization_barrier(jnp.sum(rows_grad * unit_out, axis=0))
    ffn_grad_b = norm_back(rows_grad, unit_out, root_out, g_ffn_out).astype(jnp.bfloat16)
    hidden_grad = dot32(ffn_grad_b, w_down.T)
    dgate_b = (hidden_grad * up_part * gelu_slope).astype(jnp.bfloat16)
    dup_b = (hidden_grad * gelu_value).astype(jnp.bfloat16)
    ffn_in_grad = dot32(dgate_b, w_gate) + dot32(dup_b, w_up)
    grad_w_gate = dot32(dgate_b.T, ffn_input)
    grad_w_up = dot32(dup_b.T, ffn_input)
    grad_w_down = dot32(hidden.T, ffn_grad_b)
    grad_g_ffn_in = lax.optimization_barrier(jnp.sum(ffn_in_grad * unit_ffn, axis=0))
    hidden_grad_in = rows_grad + norm_back(ffn_in_grad, unit_ffn, root_ffn, g_ffn_in)
    grad_g_attn_out = lax.optimization_barrier(jnp.sum(hidden_grad_in * unit_post, axis=0))
    attn_grad_b = norm_back(hidden_grad_in, unit_post, root_post, g_attn_out).astype(jnp.bfloat16)
    mixed_grad_b = dot32(attn_grad_b, w_out.T).astype(jnp.bfloat16)
    grad_w_out = dot32(mixed_b.T, attn_grad_b)
    mixed_grad3 = mixed_grad_b.reshape(count, HEADS, HEAD_DIM).astype(jnp.float32)
    delta = lax.optimization_barrier(jnp.sum(mixed_grad3 * mixed_b.reshape(count, HEADS, HEAD_DIM).astype(jnp.float32), axis=-1))
    value_grad = jnp.einsum('qhk,qhd->kd', probs_b.astype(jnp.float32), mixed_grad3)
    prob_grad = jnp.einsum('qhd,kd->qhk', mixed_grad3, value_b.astype(jnp.float32))
    score_grad_b = (probs * (prob_grad - delta[..., None])).astype(jnp.bfloat16)
    query_rot_grad = jnp.einsum('qhk,kd->qhd', score_grad_b.astype(jnp.float32), key_b.astype(jnp.float32)) * scale
    key_rot_grad = jnp.einsum('qhk,qhd->kd', score_grad_b.astype(jnp.float32), query_b.astype(jnp.float32)) * scale
    query_norm_grad = query_rot_grad * cos_t[:, None, :] - turn_half(query_rot_grad * sin_t[:, None, :])
    key_norm_grad = key_rot_grad * cos_t - turn_half(key_rot_grad * sin_t)
    grad_g_query = lax.optimization_barrier(jnp.sum(query_norm_grad * unit_query, axis=(0, 1)))
    grad_g_key = lax.optimization_barrier(jnp.sum(key_norm_grad * unit_key, axis=0))
    query_grad = norm_back(query_norm_grad, unit_query, root_query, g_query)
    key_grad = norm_back(key_norm_grad, unit_key, root_key, g_key)
    qkv_grad_b = jnp.concatenate([query_grad.reshape(count, qwidth), key_grad, value_grad], axis=1).astype(jnp.bfloat16)
    attn_in_grad = dot32(qkv_grad_b, w_qkv.T)
    grad_w_qkv = dot32(attn_input.T, qkv_grad_b)
    grad_g_attn_in = lax.optimization_barrier(jnp.sum(attn_in_grad * unit_attn, axis=0))
    input_grad = hidden_grad_in + norm_back(attn_in_grad, unit_attn, root_attn, g_attn_in)
    gains = jnp.stack([grad_g_attn_in, grad_g_attn_out, grad_g_ffn_in, grad_g_ffn_out])
    head_gains = jnp.stack([grad_g_query, grad_g_key])
    return ((result, input_grad), (grad_w_qkv, grad_w_out, grad_w_gate, grad_w_up, grad_w_down, gains, head_gains))

def reference(stream, stream_grad, lengths, w_qkv, w_out, w_gate, w_up, w_down, g_attn_in, g_query, g_key, g_attn_out, g_ffn_in, g_ffn_out):

    def step(totals, inputs):
        rows_in, rows_grad, lens = inputs
        outputs, grads = group_pass(rows_in, rows_grad, lens, w_qkv, w_out, w_gate, w_up, w_down, g_attn_in, g_query, g_key, g_attn_out, g_ffn_in, g_ffn_out)
        totals = tuple((first + second for first, second in zip(totals, grads)))
        return (totals, outputs)
    init = (jnp.zeros((D, (HEADS + 2) * HEAD_DIM), jnp.float32), jnp.zeros((HEADS * HEAD_DIM, D), jnp.float32), jnp.zeros((FF, D), jnp.float32), jnp.zeros((FF, D), jnp.float32), jnp.zeros((FF, D), jnp.float32), jnp.zeros((4, D), jnp.float32), jnp.zeros((2, HEAD_DIM), jnp.float32))
    totals, outputs = lax.scan(step, init, (stream, stream_grad, lengths))
    return (outputs[0], outputs[1], totals[0], totals[1], totals[2], totals[3], totals[4], totals[5][0], totals[6][0], totals[6][1], totals[5][1], totals[5][2], totals[5][3])
```

```python
import math

import functools

import jax
import jax.numpy as jnp
from jax import lax
from jax.experimental import pallas as pl
from jax.experimental.pallas import tpu as pltpu
from jax.sharding import PartitionSpec as P

HEADS = 4
HEAD_DIM = 256
WINDOW = 512


EPSILON = 1e-06
GELU_SLOPE = math.sqrt(2.0 / math.pi)
GELU_CUBIC = 0.044715


def bits_of(count):
    bits = []
    bit = 1
    while bit < count:
        bits.append(bit)
        bit *= 2
    return bits


def swapped(value, axis, bit):
    length = lax.axis_size(axis)
    return lax.ppermute(value, axis, [(i, i ^ bit) for i in range(length)])


def one_hot_order(origin, count):
    return (jnp.arange(count, dtype=jnp.int32)[:, None] == origin[None, :]).astype(jnp.bfloat16)


def in_order(value, order):
    high = value.astype(jnp.bfloat16)
    low = (value - high.astype(jnp.float32)).astype(jnp.bfloat16)
    return contract_cols(high, order) + contract_cols(low, order)


def inv_root(vector):
    return lax.rsqrt(jnp.mean(vector * vector, axis=-1, keepdims=True) + EPSILON)


def norm_back(grad, unit_part, root_part, gain):
    scaled = grad * gain
    return root_part * (scaled - unit_part * jnp.mean(scaled * unit_part, axis=-1, keepdims=True))


def gelu_pair(gate):
    inner = jnp.tanh(GELU_SLOPE * (gate + GELU_CUBIC * gate * gate * gate))
    gelu_value = 0.5 * gate * (1.0 + inner)
    gelu_slope = 0.5 * (1.0 + inner) + 0.5 * gate * (1.0 - inner * inner) * GELU_SLOPE * (
        1.0 + 3.0 * GELU_CUBIC * gate * gate
    )
    return (gelu_value, gelu_slope)


def turn_half(vector):
    half = vector.shape[-1] // 2
    return jnp.concatenate([-vector[..., half:], vector[..., :half]], axis=-1)


def seq_begin(index, starts):
    return jnp.max(jnp.where(starts[None, :] <= index[:, None], starts[None, :], 0), axis=1)


def rope_tables(position, head):
    freq = jnp.exp(-math.log(10000.0) * jnp.arange(head // 2, dtype=jnp.float32) * (2.0 / head))
    angle = position[:, None] * freq[None, :]
    angle = jnp.concatenate([angle, angle], axis=1)
    return (jnp.cos(angle), jnp.sin(angle))


def dot32(left, right):
    return jnp.dot(left, right, preferred_element_type=jnp.float32)


def contract_rows(left, right):
    return lax.dot_general(
        left, right, (((0,), (0,)), ((), ())), preferred_element_type=jnp.float32
    )


def contract_cols(left, right):
    return lax.dot_general(
        left, right, (((1,), (1,)), ((), ())), preferred_element_type=jnp.float32
    )


MESH = pl.DeviceIdType.MESH


def group_width(dp_count):
    return dp_count // 2


def flip(value, other, count):
    if count & (count - 1):
        return (value + other) % count
    total = 0
    for bit in bits_of(count):
        total = total + ((value // bit + other // bit) % 2) * bit
    return total


def column_tiles(width):
    best = 128
    for size in range(128, 513, 128):
        if width % size == 0:
            best = size
    return [slice(at, at + best) for at in range(0, width, best)]


def nt(left, right):
    return lax.dot_general(left, right, (((1,), (1,)), ((), ())), preferred_element_type=jnp.float32)


def tn(left, right):
    return lax.dot_general(left, right, (((0,), (0,)), ((), ())), preferred_element_type=jnp.float32)


def ffn_kernel(zs, ys, ws, rows, width, own, *refs):
    half = ws // 2
    x_ref, hidden_ref, grad_ref, gain_ref = refs[:4]
    w_refs = refs[4 : 4 + 3 * half]
    result_ref, gg_ref, in_grad_ref, kept_ref = refs[4 + 3 * half : 8 + 3 * half]
    at = 8 + 3 * half
    passed_ref = None
    if half > 1:
        passed_ref = refs[at]
        at += 1
    (tok, grd, wt, gate, up, hid, dgb, dub, acc, part, grad_own, ysend, yrecv, zsend, zrecv, dwsend, dwrecv) = refs[
        at : at + 17
    ]
    (agz_s, agy_s, ag_r, ry_s, ry_r, rz_s, rz_r, wl_s, wr_s, wr_r, dw_s, dw_r) = refs[at + 17 :]
    z = lax.axis_index("seq")
    d = lax.axis_index("dp")
    y = d // ws
    w = d % ws
    mate = y * ws + w + 1 - 2 * (w % 2)
    pair = ys * rows
    tiles = column_tiles(width)

    def peer(zz, yy):
        return (zz, yy * ws + w)

    def block(zz, yy):
        return pl.ds(pl.multiple_of((zz * ys + yy) * rows, rows), rows)

    def span(zz):
        return pl.ds(pl.multiple_of(zz * pair, pair), pair)

    barrier = pltpu.get_barrier_semaphore()
    for dz in range(1, zs):
        pl.semaphore_signal(barrier, inc=1, device_id=peer(flip(z, dz, zs), y), device_id_type=MESH)
    for dy in range(1, ys):
        pl.semaphore_signal(barrier, inc=1, device_id=peer(z, (y + dy) % ys), device_id_type=MESH)
    pl.semaphore_signal(barrier, inc=1, device_id=(z, mate), device_id_type=MESH)
    for i in range(half):
        for m in range(3):
            pltpu.make_async_copy(w_refs[3 * i + m], wt.at[m, 2 * i], wl_s.at[i, m]).start()
    pl.semaphore_wait(barrier, zs + ys - 1)

    def copy_z(p, src, buf, dz):
        return pltpu.make_async_remote_copy(
            src_ref=src,
            dst_ref=buf.at[block(z, y)],
            send_sem=agz_s.at[p, dz],
            recv_sem=ag_r.at[p, z, y],
            device_id=peer(flip(z, dz, zs), y),
            device_id_type=MESH,
        )

    def copy_y(p, src, buf, zz, dy):
        return pltpu.make_async_remote_copy(
            src_ref=src,
            dst_ref=buf.at[block(zz, y)],
            send_sem=agy_s.at[p, zz, dy],
            recv_sem=ag_r.at[p, zz, y],
            device_id=peer(z, (y + dy) % ys),
            device_id_type=MESH,
        )

    def arrived(p, buf, zz, yy):
        pltpu.make_async_remote_copy(
            src_ref=buf.at[block(zz, yy)],
            dst_ref=buf.at[block(zz, yy)],
            send_sem=agz_s.at[p, 0],
            recv_sem=ag_r.at[p, zz, yy],
            device_id=peer(z, y),
            device_id_type=MESH,
        ).wait_recv()

    def copy_wide(i, m):
        return pltpu.make_async_remote_copy(
            src_ref=w_refs[3 * i + m],
            dst_ref=wt.at[m, 2 * i + 1],
            send_sem=wr_s.at[i, m],
            recv_sem=wr_r.at[i, m],
            device_id=(z, mate),
            device_id_type=MESH,
        )

    def reduce_y(p, zz, dy):
        return pltpu.make_async_remote_copy(
            src_ref=ysend.at[dy - 1, zz],
            dst_ref=yrecv.at[ys - dy - 1, zz],
            send_sem=ry_s.at[p, dy - 1, zz],
            recv_sem=ry_r.at[p, ys - dy - 1, zz],
            device_id=peer(z, (y + dy) % ys),
            device_id_type=MESH,
        )

    def reduce_z(p, zz):
        return pltpu.make_async_remote_copy(
            src_ref=zsend.at[zz],
            dst_ref=zrecv.at[z],
            send_sem=rz_s.at[p, zz],
            recv_sem=rz_r.at[p, z],
            device_id=peer(zz, y),
            device_id_type=MESH,
        )

    def reduced(p, zz):
        return pltpu.make_async_remote_copy(
            src_ref=zsend.at[zz],
            dst_ref=zrecv.at[zz],
            send_sem=rz_s.at[p, zz],
            recv_sem=rz_r.at[p, zz],
            device_id=peer(z, y),
            device_id_type=MESH,
        )

    def combine(p, zz, mine):
        total = part[zz]
        for dy in range(1, ys):
            reduce_y(p, zz, dy).wait_recv()
            total = total + yrecv[ys - dy - 1, zz].astype(jnp.float32)
        if mine:
            part[zz] = total
        else:
            zsend[zz] = total.astype(jnp.bfloat16)
            reduce_z(p, zz).start()

    def phase(p, src, buf, compute, ready, between):
        for dy in range(1, ys):
            copy_y(p, src, buf, z, dy).start()
        for dz in range(1, zs):
            copy_z(p, src, buf, dz).start()
        buf[block(z, y), :] = src[...]
        ready()

        def step(dz, carry):
            zz = flip(z, dz, zs)

            @pl.when(dz + 1 < zs)
            def _():
                nxt = flip(z, dz + 1, zs)
                arrived(p, buf, nxt, y)
                for dy in range(1, ys):
                    copy_y(p, buf.at[block(nxt, y)], buf, nxt, dy).start()

            for dy in range(1, ys):
                arrived(p, buf, zz, (y + dy) % ys)
            compute(zz)
            for dy in range(1, ys):
                yy = (y + dy) % ys
                ysend[dy - 1, zz] = acc[pl.ds(pl.multiple_of(yy * rows, rows), rows), :].astype(jnp.bfloat16)
                reduce_y(p, zz, dy).start()
            part[zz] = acc[pl.ds(pl.multiple_of(y * rows, rows), rows), :]

            @pl.when(dz == 1)
            def _():
                combine(p, z, True)

            @pl.when(dz > 1)
            def _():
                combine(p, flip(z, dz - 1, zs), False)

            return carry

        lax.fori_loop(0, zs, step, 0)
        combine(p, flip(z, zs - 1, zs), zs == 1)
        between()
        total = part[z]
        for dz in range(1, zs):
            zz = flip(z, dz, zs)
            reduced(p, zz).wait_recv()
            total = total + zrecv[zz].astype(jnp.float32)
        return total

    def sent(p, src, buf):
        for dz in range(1, zs):
            copy_z(p, src, buf, dz).wait_send()
            reduce_z(p, flip(z, dz, zs)).wait_send()
        for zz in range(zs):
            for dy in range(1, ys):
                copy_y(p, src, buf, zz, dy).wait_send()
                reduce_y(p, zz, dy).wait_send()

    def forward(zz):
        acc[...] = jnp.zeros_like(acc)

        def shard(s, carry):
            x = tok[span(zz), :]
            gate_part = nt(x, wt[0, s])
            up_part = nt(x, wt[1, s])
            gate[s, span(zz), :] = gate_part
            up[s, span(zz), :] = up_part
            inner = jnp.tanh(GELU_SLOPE * (gate_part + GELU_CUBIC * gate_part * gate_part * gate_part))
            hidden = (0.5 * gate_part * (1.0 + inner) * up_part).astype(jnp.bfloat16)
            hid[s, span(zz), :] = hidden
            for tile in tiles:
                acc[:, tile] = acc[:, tile] + dot32(hidden, wt[2, s, :, tile])
            return carry

        lax.fori_loop(0, ws, shard, 0)

    def backward(zz):
        acc[...] = jnp.zeros_like(acc)

        def shard(s, carry):
            hidden_grad = nt(grd[span(zz), :], wt[2, s])
            gelu_value, gelu_slope = gelu_pair(gate[s, span(zz), :])
            dgate = (hidden_grad * up[s, span(zz), :] * gelu_slope).astype(jnp.bfloat16)
            dup = (hidden_grad * gelu_value).astype(jnp.bfloat16)
            dgb[s, span(zz), :] = dgate
            dub[s, span(zz), :] = dup
            for tile in tiles:
                acc[:, tile] = acc[:, tile] + dot32(dgate, wt[0, s, :, tile]) + dot32(dup, wt[1, s, :, tile])
            return carry

        lax.fori_loop(0, ws, shard, 0)

    def weights_ready():
        for i in range(half):
            for m in range(3):
                pltpu.make_async_copy(w_refs[3 * i + m], wt.at[m, 2 * i], wl_s.at[i, m]).wait()
        for i in range(half):
            for m in range(3):
                copy_wide(i, m).wait_recv()

    def nothing():
        return None

    def copy_dw(i, m):
        return pltpu.make_async_remote_copy(
            src_ref=dwsend.at[i, m],
            dst_ref=dwrecv.at[i, m],
            send_sem=dw_s.at[i, m],
            recv_sem=dw_r.at[i, m],
            device_id=(z, mate),
            device_id_type=MESH,
        )

    terms = ((dgb, tok), (dub, tok), (hid, grd))

    def weight_terms():
        for m in range(3):
            left, right = terms[m]

            def away(i, carry):
                for tile in tiles:
                    dwsend[i, m, :, tile] = tn(left[2 * i + 1], right[:, tile]).astype(jnp.bfloat16)
                copy_dw(i, m).start()
                return carry

            lax.fori_loop(0, half, away, 0)
        for m in range(3):
            left, right = terms[m]

            def home(i, carry):
                copy_dw(i, m).wait_recv()
                for tile in tiles:
                    total = tn(left[2 * i], right[:, tile]) + dwrecv[i, m, :, tile].astype(jnp.float32)

                    @pl.when(i == 0)
                    def _():
                        kept_ref[m, :, tile] = total

                    if half > 1:

                        @pl.when(i > 0)
                        def _():
                            passed_ref[jnp.maximum(i - 1, 0), m, :, tile] = total.astype(jnp.bfloat16)

                return carry

            lax.fori_loop(0, half, home, 0)

    for i in range(half):
        for m in range(3):
            copy_wide(i, m).start()
    ffn_out = phase(0, x_ref, tok, forward, weights_ready, nothing)
    root = inv_root(ffn_out)
    unit = ffn_out * root
    gain = gain_ref[...]
    result_ref[...] = hidden_ref[...] + unit * gain
    rows_grad = grad_ref[...]
    gg_ref[...] = jnp.sum(rows_grad * unit, axis=0, keepdims=True)
    grad_own[...] = norm_back(rows_grad, unit, root, gain).astype(jnp.bfloat16)
    sent(0, x_ref, tok)
    in_grad_ref[...] = phase(1, grad_own, grd, backward, nothing, weight_terms)

    for i in range(half):
        for m in range(3):
            copy_wide(i, m).wait_send()
            copy_dw(i, m).wait_send()
    sent(1, grad_own, grd)


def ffn_block(ffn_input, hidden_in, rows_grad, gain, ffn_rows, zs, dp_count):
    rows, width = ffn_input.shape
    own = ffn_rows[0][0].shape[0]
    ws = group_width(dp_count)
    ys = dp_count // ws
    half = ws // 2
    tokens = zs * ys * rows
    bf, f32 = jnp.bfloat16, jnp.float32
    vmem = pl.BlockSpec(memory_space=pltpu.VMEM)
    outs = [
        jax.ShapeDtypeStruct((rows, width), f32),
        jax.ShapeDtypeStruct((1, width), f32),
        jax.ShapeDtypeStruct((rows, width), f32),
        jax.ShapeDtypeStruct((3, own, width), f32),
    ]
    if half > 1:
        outs.append(jax.ShapeDtypeStruct((half - 1, 3, own, width), bf))
    dma = pltpu.SemaphoreType.DMA
    scratch = [
        pltpu.VMEM((tokens, width), bf),
        pltpu.VMEM((tokens, width), bf),
        pltpu.VMEM((3, ws, own, width), bf),
        pltpu.VMEM((ws, tokens, own), f32),
        pltpu.VMEM((ws, tokens, own), f32),
        pltpu.VMEM((ws, tokens, own), bf),
        pltpu.VMEM((ws, tokens, own), bf),
        pltpu.VMEM((ws, tokens, own), bf),
        pltpu.VMEM((ys * rows, width), f32),
        pltpu.VMEM((zs, rows, width), f32),
        pltpu.VMEM((rows, width), bf),
        pltpu.VMEM((ys - 1, zs, rows, width), bf),
        pltpu.VMEM((ys - 1, zs, rows, width), bf),
        pltpu.VMEM((zs, rows, width), bf),
        pltpu.VMEM((zs, rows, width), bf),
        pltpu.VMEM((half, 3, own, width), bf),
        pltpu.VMEM((half, 3, own, width), bf),
        dma((2, zs)),
        dma((2, zs, ys)),
        dma((2, zs, ys)),
        dma((2, ys - 1, zs)),
        dma((2, ys - 1, zs)),
        dma((2, zs)),
        dma((2, zs)),
        dma((half, 3)),
        dma((half, 3)),
        dma((half, 3)),
        dma((half, 3)),
        dma((half, 3)),
    ]
    flat = [w for group in ffn_rows for w in group]
    flops = 2 * tokens * ws * own * width * 9
    out = pl.pallas_call(
        functools.partial(ffn_kernel, zs, ys, ws, rows, width, own),
        out_shape=outs,
        in_specs=[vmem] * 4 + [pl.BlockSpec(memory_space=pl.ANY)] * len(flat),
        out_specs=[vmem] * len(outs),
        scratch_shapes=scratch,
        compiler_params=pltpu.CompilerParams(
            collective_id=1, has_side_effects=True, vmem_limit_bytes=67043328
        ),
        cost_estimate=pl.CostEstimate(flops=flops, bytes_accessed=40 << 20, transcendentals=0),
        name="ffn_block",
    )(ffn_input, hidden_in, rows_grad, gain[None, :], *flat)
    passed = out[4] if half > 1 else None
    return out[0], out[1], out[2], out[3], passed


def spread_kernel(zs, ys, xs, width, cut, with_kv, *refs):
    refs = list(refs)
    w_ref = refs.pop(0)
    kv_ref = refs.pop(0) if with_kv else None
    out_ref = refs.pop(0)
    kv_out = refs.pop(0) if with_kv else None
    own_s, z_s, far_s, far_r = refs[:4]
    kv_own, kv_s, kv_r = refs[4:7] if with_kv else (None, None, None)
    z = lax.axis_index("seq")
    d = lax.axis_index("dp")
    y, x, c = d // (2 * xs), (d // 2) % xs, d % 2
    cols = (pl.ds(0, cut), pl.ds(cut, width - cut))

    def dev(zz, yy, xx, cc):
        return (zz, (yy * xs + xx) * 2 + cc)

    barrier = pltpu.get_barrier_semaphore()
    near = [dev(flip(z, dz, zs), y, x, c) for dz in range(1, zs)]
    near += [dev(z, (y + dy) % ys, x, c) for dy in range(1, ys)]
    near += [dev(z, y, (x + dx) % xs, c) for dx in range(1, xs)]
    near += [dev(z, y, x, 1 - c)]
    for peer in near:
        pl.semaphore_signal(barrier, inc=1, device_id=peer, device_id_type=MESH)
    pl.semaphore_wait(barrier, len(near))

    def slot(h, zz, yy, xx, cc):
        return out_ref.at[zz, yy, xx, cc, :, cols[h]]

    def copy(h, src, zz, yy, xx, send, to):
        return pltpu.make_async_remote_copy(
            src_ref=src,
            dst_ref=slot(h, zz, yy, xx, c),
            send_sem=send,
            recv_sem=far_r.at[h, zz, yy, xx, c],
            device_id=to,
            device_id_type=MESH,
        )

    def along(h, dz):
        return copy(h, w_ref.at[:, cols[h]], z, y, x, z_s.at[h, dz], dev(flip(z, dz, zs), y, x, c))

    def over_y(h, src, zz, yy, xx, dy):
        return copy(h, src, zz, yy, xx, far_s.at[h, zz, yy, xx, dy], dev(z, (y + dy) % ys, x, c))

    def over_x(h, src, zz, yy, xx, dx):
        return copy(h, src, zz, yy, xx, far_s.at[h, zz, yy, xx, ys - 1 + dx], dev(z, y, (x + dx) % xs, c))

    def over_core(h, src, zz, yy, xx):
        return copy(h, src, zz, yy, xx, far_s.at[h, zz, yy, xx, 0], dev(z, y, x, 1 - c))

    def arrived(h, zz, yy, xx, cc):
        pltpu.make_async_remote_copy(
            src_ref=slot(h, zz, yy, xx, cc),
            dst_ref=slot(h, zz, yy, xx, cc),
            send_sem=z_s.at[h, 0],
            recv_sem=far_r.at[h, zz, yy, xx, cc],
            device_id=dev(z, y, x, 1 - c),
            device_id_type=MESH,
        ).wait_recv()

    def kv_copy(dz):
        return pltpu.make_async_remote_copy(
            src_ref=kv_ref,
            dst_ref=kv_out.at[z],
            send_sem=kv_s.at[dz],
            recv_sem=kv_r.at[z],
            device_id=dev(flip(z, dz, zs), y, x, c),
            device_id_type=MESH,
        )

    def kv_arrived(zz):
        pltpu.make_async_remote_copy(
            src_ref=kv_ref,
            dst_ref=kv_out.at[zz],
            send_sem=kv_s.at[0],
            recv_sem=kv_r.at[zz],
            device_id=dev(z, y, x, 1 - c),
            device_id_type=MESH,
        ).wait_recv()

    def onward(h, src, zz):
        if h == 0:
            for dy in range(1, ys):
                over_y(h, src, zz, y, x, dy).start()
        for dx in range(1, xs):
            over_x(h, src, zz, y, x, dx).start()
        if h == 1:
            for dy in range(1, ys):
                over_y(h, src, zz, y, x, dy).start()
        over_core(h, src, zz, y, x).start()

    if with_kv:
        for dz in range(1, zs):
            kv_copy(dz).start()
    for dz in range(1, zs):
        for h in range(2):
            along(h, dz).start()
    for h in range(2):
        onward(h, w_ref.at[:, cols[h]], z)
    keep = pltpu.make_async_copy(w_ref, out_ref.at[z, y, x, c], own_s.at[0])
    keep.start()
    if with_kv:
        kv_keep = pltpu.make_async_copy(kv_ref, kv_out.at[z], kv_own.at[0])
        kv_keep.start()

    def step(t, carry):
        @pl.when(t < zs)
        def _():
            zz = flip(z, t, zs)
            for h in range(2):

                @pl.when(t > 0)
                def _():
                    arrived(h, zz, y, x, c)
                    onward(h, slot(h, zz, y, x, c), zz)

        @pl.when(jnp.logical_and(t >= 1, t < zs + 1))
        def _():
            zz = flip(z, t - 1, zs)
            for dy in range(1, ys):
                yy = (y + dy) % ys
                arrived(0, zz, yy, x, c)
                for dx in range(1, xs):
                    over_x(0, slot(0, zz, yy, x, c), zz, yy, x, dx).start()
                over_core(0, slot(0, zz, yy, x, c), zz, yy, x).start()
            for dx in range(1, xs):
                xx = (x + dx) % xs
                arrived(1, zz, y, xx, c)
                for dy in range(1, ys):
                    over_y(1, slot(1, zz, y, xx, c), zz, y, xx, dy).start()
                over_core(1, slot(1, zz, y, xx, c), zz, y, xx).start()

        @pl.when(t >= 2)
        def _():
            zz = flip(z, t - 2, zs)
            for dx in range(1, xs):
                xx = (x + dx) % xs
                for dy in range(ys):
                    yy = (y + dy) % ys
                    arrived(0, zz, yy, xx, c)
                    over_core(0, slot(0, zz, yy, xx, c), zz, yy, xx).start()
            for dy in range(1, ys):
                yy = (y + dy) % ys
                for dx in range(xs):
                    xx = (x + dx) % xs
                    arrived(1, zz, yy, xx, c)
                    over_core(1, slot(1, zz, yy, xx, c), zz, yy, xx).start()

        return carry

    lax.fori_loop(0, zs + 2, step, 0)

    def settle(zz, carry):
        for yy in range(ys):
            for xx in range(xs):
                for h in range(2):
                    arrived(h, zz, yy, xx, 1 - c)
                    over_core(h, slot(h, zz, yy, xx, c), zz, yy, xx).wait_send()
        for dx in range(1, xs):
            for dy in range(ys):
                yy = (y + dy) % ys
                over_x(0, slot(0, zz, yy, x, c), zz, yy, x, dx).wait_send()
            over_x(1, slot(1, zz, y, x, c), zz, y, x, dx).wait_send()
        for dy in range(1, ys):
            for dx in range(xs):
                xx = (x + dx) % xs
                over_y(1, slot(1, zz, y, xx, c), zz, y, xx, dy).wait_send()
            over_y(0, slot(0, zz, y, x, c), zz, y, x, dy).wait_send()
        return carry

    lax.fori_loop(0, zs, settle, 0)
    keep.wait()
    for dz in range(1, zs):
        for h in range(2):
            along(h, dz).wait_send()
    if with_kv:
        kv_keep.wait()
        for dz in range(1, zs):
            kv_arrived(flip(z, dz, zs))
            kv_copy(dz).wait_send()


def half_columns(width):
    return (width // 256) * 128 + (128 if width % 256 else 0)


def spread(block, kv, zs, dp_count, ident):
    own, width = block.shape
    ys, xs = 2, dp_count // 4
    bf = jnp.bfloat16
    dma = pltpu.SemaphoreType.DMA
    vmem, hbm = pl.BlockSpec(memory_space=pltpu.VMEM), pl.BlockSpec(memory_space=pl.ANY)
    outs = [jax.ShapeDtypeStruct((zs, ys, xs, 2, own, width), bf)]
    scratch = [dma((1,)), dma((2, zs)), dma((2, zs, ys, xs, ys + xs - 1)), dma((2, zs, ys, xs, 2))]
    args = [block]
    if kv is not None:
        args.append(kv)
        outs.append(jax.ShapeDtypeStruct((zs,) + kv.shape, bf))
        scratch += [dma((1,)), dma((zs,)), dma((zs,))]
    out = pl.pallas_call(
        functools.partial(spread_kernel, zs, ys, xs, width, half_columns(width), kv is not None),
        out_shape=outs,
        in_specs=[vmem] * len(args),
        out_specs=[hbm] * len(outs),
        scratch_shapes=scratch,
        compiler_params=pltpu.CompilerParams(collective_id=ident, has_side_effects=True),
        cost_estimate=pl.CostEstimate(flops=1 << 20, bytes_accessed=24 << 20, transcendentals=0),
        name="spread",
    )(*args)
    return out[0].reshape(-1, own, width), (out[1] if kv is not None else None)


def fold_kernel(zs, ys, xs, width, cut, with_kv, *refs):
    refs = list(refs)
    term = refs.pop(0)
    kv_ref = refs.pop(0) if with_kv else None
    out_ref = refs.pop(0)
    kv_out = refs.pop(0) if with_kv else None
    (crecv, s1, r2a, s2a, r3a, s3a, r4a, r2b, s2b, r3b, s3b, r4b, c_s, c_r) = refs[:14]
    (a2_s, a2_r, a3_s, a3_r, a4_s, a4_r, b2_s, b2_r, b3_s, b3_r, b4_s, b4_r) = refs[14:26]
    kv_got, kv_s, kv_r = refs[26:29] if with_kv else (None, None, None)
    z = lax.axis_index("seq")
    d = lax.axis_index("dp")
    y, x, c = d // (2 * xs), (d // 2) % xs, d % 2
    left, right = pl.ds(0, cut), pl.ds(cut, width - cut)
    f32, bf = jnp.float32, jnp.bfloat16

    def dev(zz, yy, xx, cc):
        return (zz, (yy * xs + xx) * 2 + cc)

    barrier = pltpu.get_barrier_semaphore()
    near = [dev(flip(z, dz, zs), y, x, c) for dz in range(1, zs)]
    near += [dev(z, (y + dy) % ys, x, c) for dy in range(1, ys)]
    near += [dev(z, y, (x + dx) % xs, c) for dx in range(1, xs)]
    near += [dev(z, y, x, 1 - c)]
    for peer in near:
        pl.semaphore_signal(barrier, inc=1, device_id=peer, device_id_type=MESH)
    pl.semaphore_wait(barrier, len(near))

    def remote(src, dst, send, recv, to):
        return pltpu.make_async_remote_copy(
            src_ref=src, dst_ref=dst, send_sem=send, recv_sem=recv, device_id=to, device_id_type=MESH
        )

    def core_copy(zz, yy, xx):
        return remote(
            term.at[zz, yy, xx, 1 - c], crecv.at[zz, yy, xx], c_s.at[zz, yy, xx], c_r.at[zz, yy, xx], dev(z, y, x, 1 - c)
        )

    def kv_copy(dz):
        zz = flip(z, dz, zs)
        return remote(kv_ref.at[zz], kv_got.at[dz], kv_s.at[dz], kv_r.at[dz], dev(zz, y, x, c))

    def a2(zz, yy, dx):
        to = dev(z, y, (x + dx) % xs, c)
        src = s1.at[zz, yy, (x + dx) % xs, :, left]
        return remote(src, r2a.at[xs - dx - 1, zz, yy], a2_s.at[dx - 1, zz, yy], a2_r.at[xs - dx - 1, zz, yy], to)

    def b2(zz, xx, dy):
        to = dev(z, (y + dy) % ys, x, c)
        src = s1.at[zz, (y + dy) % ys, xx, :, right]
        return remote(src, r2b.at[ys - dy - 1, zz, xx], b2_s.at[dy - 1, zz, xx], b2_r.at[ys - dy - 1, zz, xx], to)

    def a3(zz, dy):
        to = dev(z, (y + dy) % ys, x, c)
        src = s2a.at[zz, (y + dy) % ys]
        return remote(src, r3a.at[ys - dy - 1, zz], a3_s.at[dy - 1, zz], a3_r.at[ys - dy - 1, zz], to)

    def b3(zz, dx):
        to = dev(z, y, (x + dx) % xs, c)
        src = s2b.at[zz, (x + dx) % xs]
        return remote(src, r3b.at[xs - dx - 1, zz], b3_s.at[dx - 1, zz], b3_r.at[xs - dx - 1, zz], to)

    def a4(dz):
        zz = flip(z, dz, zs)
        return remote(s3a.at[dz], r4a.at[dz], a4_s.at[dz], a4_r.at[dz], dev(zz, y, x, c))

    def b4(dz):
        zz = flip(z, dz, zs)
        return remote(s3b.at[dz], r4b.at[dz], b4_s.at[dz], b4_r.at[dz], dev(zz, y, x, c))

    if with_kv:
        for dz in range(1, zs):
            kv_copy(dz).start()

    def first(t, carry):
        zz = flip(z, zs - 1 - t, zs)
        for yy in range(ys):
            for xx in range(xs):
                core_copy(zz, yy, xx).start()
        return carry

    lax.fori_loop(0, zs, first, 0)

    def step(t, carry):
        @pl.when(t < zs)
        def _():
            zz = flip(z, zs - 1 - t, zs)
            for yy in range(ys):
                for xx in range(xs):
                    core_copy(zz, yy, xx).wait_recv()
                    total = term[zz, yy, xx, c].astype(f32) + crecv[zz, yy, xx].astype(f32)
                    s1[zz, yy, xx] = total.astype(bf)
            for dx in range(1, xs):
                for yy in range(ys):
                    a2(zz, yy, dx).start()
            for dy in range(1, ys):
                for xx in range(xs):
                    b2(zz, xx, dy).start()

        @pl.when(jnp.logical_and(t >= 1, t < zs + 1))
        def _():
            zz = flip(z, zs - t, zs)
            for yy in range(ys):
                total = s1[zz, yy, x, :, left].astype(f32)
                for dx in range(1, xs):
                    a2(zz, yy, dx).wait_recv()
                    total = total + r2a[xs - dx - 1, zz, yy].astype(f32)
                s2a[zz, yy] = total.astype(bf)
            for dy in range(1, ys):
                a3(zz, dy).start()
            for xx in range(xs):
                total = s1[zz, y, xx, :, right].astype(f32)
                for dy in range(1, ys):
                    b2(zz, xx, dy).wait_recv()
                    total = total + r2b[ys - dy - 1, zz, xx].astype(f32)
                s2b[zz, xx] = total.astype(bf)
            for dx in range(1, xs):
                b3(zz, dx).start()

        @pl.when(t >= 2)
        def _():
            dz = zs + 1 - t
            zz = flip(z, dz, zs)
            total = s2a[zz, y].astype(f32)
            for dy in range(1, ys):
                a3(zz, dy).wait_recv()
                total = total + r3a[ys - dy - 1, zz].astype(f32)
            other = s2b[zz, x].astype(f32)
            for dx in range(1, xs):
                b3(zz, dx).wait_recv()
                other = other + r3b[xs - dx - 1, zz].astype(f32)

            @pl.when(dz > 0)
            def _():
                s3a[dz] = total.astype(bf)
                a4(dz).start()
                s3b[dz] = other.astype(bf)
                b4(dz).start()

            @pl.when(dz == 0)
            def _():
                out_ref[:, left] = total
                out_ref[:, right] = other

        return carry

    lax.fori_loop(0, zs + 2, step, 0)
    total = out_ref[:, left]
    other = out_ref[:, right]
    for dz in range(1, zs):
        a4(dz).wait_recv()
        total = total + r4a[dz].astype(f32)
        b4(dz).wait_recv()
        other = other + r4b[dz].astype(f32)
    out_ref[:, left] = total
    out_ref[:, right] = other
    if with_kv:
        kv_total = kv_ref[z].astype(f32)
        for dz in range(1, zs):
            kv_copy(dz).wait_recv()
            kv_total = kv_total + kv_got[dz].astype(f32)
        kv_out[...] = kv_total
        for dz in range(1, zs):
            kv_copy(dz).wait_send()

    def settle(zz, carry):
        for yy in range(ys):
            for xx in range(xs):
                core_copy(zz, yy, xx).wait_send()
        for dx in range(1, xs):
            for yy in range(ys):
                a2(zz, yy, dx).wait_send()
            b3(zz, dx).wait_send()
        for dy in range(1, ys):
            for xx in range(xs):
                b2(zz, xx, dy).wait_send()
            a3(zz, dy).wait_send()
        return carry

    lax.fori_loop(0, zs, settle, 0)
    for dz in range(1, zs):
        a4(dz).wait_send()
        b4(dz).wait_send()


def fold(term, kv, zs, dp_count, ident):
    own, width = term.shape[1:]
    ys, xs = 2, dp_count // 4
    cut = half_columns(width)
    rest = width - cut
    bf, f32 = jnp.bfloat16, jnp.float32
    dma = pltpu.SemaphoreType.DMA
    vmem = pl.BlockSpec(memory_space=pltpu.VMEM)
    outs = [jax.ShapeDtypeStruct((own, width), f32)]
    args = [term.reshape(zs, ys, xs, 2, own, width)]
    sizes = [
        (zs, ys, xs, own, width),
        (zs, ys, xs, own, width),
        (xs - 1, zs, ys, own, cut),
        (zs, ys, own, cut),
        (ys - 1, zs, own, cut),
        (zs, own, cut),
        (zs, own, cut),
        (ys - 1, zs, xs, own, rest),
        (zs, xs, own, rest),
        (xs - 1, zs, own, rest),
        (zs, own, rest),
        (zs, own, rest),
    ]
    scratch = [pltpu.VMEM(size, bf) for size in sizes]
    scratch += [dma((zs, ys, xs))] * 2
    scratch += [dma((xs - 1, zs, ys))] * 2 + [dma((ys - 1, zs))] * 2 + [dma((zs,))] * 2
    scratch += [dma((ys - 1, zs, xs))] * 2 + [dma((xs - 1, zs))] * 2 + [dma((zs,))] * 2
    if kv is not None:
        args.append(kv)
        outs.append(jax.ShapeDtypeStruct(kv.shape[1:], f32))
        scratch += [pltpu.VMEM(kv.shape, bf), dma((zs,)), dma((zs,))]
    out = pl.pallas_call(
        functools.partial(fold_kernel, zs, ys, xs, width, cut, kv is not None),
        out_shape=outs,
        in_specs=[vmem] * len(args),
        out_specs=[vmem] * len(outs),
        scratch_shapes=scratch,
        compiler_params=pltpu.CompilerParams(collective_id=ident, has_side_effects=True),
        cost_estimate=pl.CostEstimate(flops=1 << 20, bytes_accessed=24 << 20, transcendentals=0),
        name="fold",
    )(*args)
    return out[0], (out[1] if kv is not None else None)


def local(
    stream,
    stream_grad,
    lengths,
    w_qkv,
    w_out,
    w_gate,
    w_up,
    w_down,
    g_attn_in,
    g_query,
    g_key,
    g_attn_out,
    g_ffn_in,
    g_ffn_out,
):
    rows_in = stream[0]
    rows_grad = stream_grad[0]
    lens = lengths[0]
    rows = rows_in.shape[0]
    width = rows_in.shape[1]
    qwidth = HEADS * HEAD_DIM
    seq_count = lax.axis_size("seq")
    dp_count = lax.axis_size("dp")
    count = seq_count * dp_count
    keys = seq_count * rows
    scale = 1.0 / math.sqrt(HEAD_DIM)
    block_id = lax.axis_index("seq")
    qkv_own = w_qkv.shape[0]
    qkv_pad = (qkv_own + 8) // 8 * 8
    lane = jnp.arange(qkv_pad, dtype=jnp.int32)[None, :]
    owner = jnp.arange(count, dtype=jnp.int32)[:, None]
    qkv_origin = jnp.where(lane < qkv_own, owner * qkv_own + lane, -1).reshape(-1)
    qkv_order = one_hot_order(qkv_origin, width)
    w_qkv_pad = jnp.pad(w_qkv, ((0, qkv_pad - qkv_own), (0, 0)))
    qkv_full, _ = spread(w_qkv_pad, None, seq_count, dp_count, 2)
    qkv_full = qkv_full.reshape(count * qkv_pad, -1)
    groups = group_width(dp_count)
    ffn_rows = [(w_gate, w_up, w_down)] + [
        tuple(swapped(w, "dp", 2 * i) for w in (w_gate, w_up, w_down)) for i in range(1, groups // 2)
    ]
    starts = jnp.cumsum(lens) - lens
    own_index = block_id * rows + jnp.arange(rows, dtype=jnp.int32)
    key_index = jnp.arange(keys, dtype=jnp.int32)
    own_begin = seq_begin(own_index, starts)
    key_begin = seq_begin(key_index, starts)
    mask = (
        (key_begin[None, :] == own_begin[:, None])
        & (key_index[None, :] <= own_index[:, None])
        & (own_index[:, None] - key_index[None, :] < WINDOW)
    )
    full_mask = mask[:, None, :]
    cos_t, sin_t = rope_tables((own_index - own_begin).astype(jnp.float32), HEAD_DIM)
    root_attn = inv_root(rows_in)
    unit_attn = rows_in * root_attn
    attn_input = (unit_attn * g_attn_in).astype(jnp.bfloat16)
    attn_slots = dot32(attn_input, qkv_order).astype(jnp.bfloat16)
    projected = dot32(attn_slots, qkv_full)
    query = projected[:, :qwidth].reshape(rows, HEADS, HEAD_DIM)
    key_raw = projected[:, qwidth : qwidth + HEAD_DIM]
    value_raw = projected[:, qwidth + HEAD_DIM :]
    root_query = inv_root(query)
    unit_query = query * root_query
    query_norm = unit_query * g_query
    root_key = inv_root(key_raw)
    unit_key = key_raw * root_key
    key_norm = unit_key * g_key
    query_rot = query_norm * cos_t[:, None, :] + turn_half(query_norm) * sin_t[:, None, :]
    key_rot = key_norm * cos_t + turn_half(key_norm) * sin_t
    query_b = query_rot.astype(jnp.bfloat16)
    kv_own = jnp.concatenate([key_rot.astype(jnp.bfloat16), value_raw.astype(jnp.bfloat16)], axis=1)
    out_full, kv_all = spread(w_out, kv_own, seq_count, dp_count, 3)
    out_full = out_full.reshape(qwidth, width)
    kv_all = kv_all.reshape(keys, 2 * HEAD_DIM)
    keys_b = kv_all[:, :HEAD_DIM]
    values_b = kv_all[:, HEAD_DIM:]
    scores = jnp.einsum("rhd,kd->rhk", query_b, keys_b, preferred_element_type=jnp.float32) * scale
    logsum = jnp.log(jnp.sum(jnp.where(full_mask, jnp.exp(scores), 0.0), axis=-1))
    probs = jnp.where(full_mask, jnp.exp(scores - logsum[..., None]), 0.0)
    probs_b = probs.astype(jnp.bfloat16)
    mixed = jnp.einsum("rhk,kd->rhd", probs_b, values_b, preferred_element_type=jnp.float32)
    mixed_b = mixed.reshape(rows, qwidth).astype(jnp.bfloat16)
    attn_out = dot32(mixed_b, out_full)
    root_post = inv_root(attn_out)
    unit_post = attn_out * root_post
    hidden_in = rows_in + unit_post * g_attn_out
    root_ffn = inv_root(hidden_in)
    unit_ffn = hidden_in * root_ffn
    ffn_input = (unit_ffn * g_ffn_in).astype(jnp.bfloat16)

    result, grad_g_ffn_out, ffn_in_grad, kept, passed = ffn_block(
        ffn_input, hidden_in, rows_grad, g_ffn_out, ffn_rows, seq_count, dp_count
    )
    grad_g_ffn_out = grad_g_ffn_out[0]
    for i in range(1, groups // 2):
        kept = kept + swapped(passed[i - 1], "dp", 2 * i).astype(jnp.float32)
    grad_w_gate, grad_w_up, grad_w_down = kept[0], kept[1], kept[2]
    grad_g_ffn_in = jnp.sum(ffn_in_grad * unit_ffn, axis=0)
    hidden_grad_in = rows_grad + norm_back(ffn_in_grad, unit_ffn, root_ffn, g_ffn_in)
    grad_g_attn_out = jnp.sum(hidden_grad_in * unit_post, axis=0)
    attn_grad_b = norm_back(hidden_grad_in, unit_post, root_post, g_attn_out).astype(jnp.bfloat16)
    mixed_grad_b = contract_cols(attn_grad_b, out_full).astype(jnp.bfloat16)
    out_term = contract_rows(mixed_b, attn_grad_b).astype(jnp.bfloat16).reshape((count,) + w_out.shape)
    mixed_grad3 = mixed_grad_b.reshape(rows, HEADS, HEAD_DIM)
    delta = jnp.sum(
        mixed_grad3.astype(jnp.float32)
        * mixed_b.reshape(rows, HEADS, HEAD_DIM).astype(jnp.float32),
        axis=-1,
    )
    scores_again = (
        jnp.einsum("rhd,kd->rhk", query_b, keys_b, preferred_element_type=jnp.float32) * scale
    )
    probs_again = jnp.where(full_mask, jnp.exp(scores_again - logsum[..., None]), 0.0)
    probs_again_b = probs_again.astype(jnp.bfloat16)
    value_grad_all = jnp.einsum(
        "rhk,rhd->kd", probs_again_b, mixed_grad3, preferred_element_type=jnp.float32
    )
    prob_grad = jnp.einsum("rhd,kd->rhk", mixed_grad3, values_b, preferred_element_type=jnp.float32)
    score_grad_b = (probs_again * (prob_grad - delta[..., None])).astype(jnp.bfloat16)
    query_rot_grad = (
        jnp.einsum("rhk,kd->rhd", score_grad_b, keys_b, preferred_element_type=jnp.float32) * scale
    )
    key_grad_all = (
        jnp.einsum("rhk,rhd->kd", score_grad_b, query_b, preferred_element_type=jnp.float32) * scale
    )
    kv_grad_all = jnp.concatenate([key_grad_all, value_grad_all], axis=1)
    owned_out, kv_grad = fold(
        out_term, kv_grad_all.astype(jnp.bfloat16).reshape(seq_count, rows, -1), seq_count, dp_count, 4
    )
    key_rot_grad = kv_grad[:, :HEAD_DIM]
    value_grad = kv_grad[:, HEAD_DIM:]
    query_norm_grad = query_rot_grad * cos_t[:, None, :] - turn_half(
        query_rot_grad * sin_t[:, None, :]
    )
    key_norm_grad = key_rot_grad * cos_t - turn_half(key_rot_grad * sin_t)
    grad_g_query = jnp.sum(query_norm_grad * unit_query, axis=(0, 1))
    grad_g_key = jnp.sum(key_norm_grad * unit_key, axis=0)
    query_grad = norm_back(query_norm_grad, unit_query, root_query, g_query)
    key_grad = norm_back(key_norm_grad, unit_key, root_key, g_key)
    qkv_grad_b = jnp.concatenate(
        [query_grad.reshape(rows, qwidth), key_grad, value_grad], axis=1
    ).astype(jnp.bfloat16)
    attn_in_grad = in_order(contract_cols(qkv_grad_b, qkv_full), qkv_order)
    grad_g_attn_in = jnp.sum(attn_in_grad * unit_attn, axis=0)
    input_grad = hidden_grad_in + norm_back(attn_in_grad, unit_attn, root_attn, g_attn_in)
    gains = [grad_g_attn_in, grad_g_attn_out, grad_g_ffn_in, grad_g_ffn_out, grad_g_query, grad_g_key]
    gain_terms = jnp.concatenate([g.reshape(count, -1) for g in gains], axis=1)
    qkv_term = contract_rows(attn_slots, qkv_grad_b).astype(jnp.bfloat16).reshape(count, qkv_pad, -1)
    gain_rows = jnp.pad(gain_terms, ((0, 0), (0, w_qkv.shape[1] - gain_terms.shape[1]))).astype(jnp.bfloat16)
    qkv_term = jnp.where(
        jnp.arange(qkv_pad, dtype=jnp.int32)[None, :, None] == qkv_own, gain_rows[:, None, :], qkv_term
    )
    owned_all, _ = fold(qkv_term, None, seq_count, dp_count, 5)
    owned_qkv = owned_all[:qkv_own]
    owned = owned_all[qkv_own]
    own_width, own_head = width // count, HEAD_DIM // count
    owned_gains = [owned[i * own_width : (i + 1) * own_width] for i in range(4)]
    owned_heads = [
        owned[4 * own_width + i * own_head : 4 * own_width + (i + 1) * own_head] for i in range(2)
    ]
    return (
        result[None],
        input_grad[None],
        owned_qkv,
        owned_out,
        grad_w_gate,
        grad_w_up,
        grad_w_down,
        owned_gains[0],
        owned_heads[0],
        owned_heads[1],
        owned_gains[1],
        owned_gains[2],
        owned_gains[3],
    )


def solution(mesh):
    return jax.shard_map(
        local,
        mesh=mesh,
        in_specs=(
            P("dp", "seq", None),
            P("dp", "seq", None),
            P("dp", None),
            P(("seq", "dp"), None),
            P(("seq", "dp"), None),
            P(("seq", "dp"), None),
            P(("seq", "dp"), None),
            P(("seq", "dp"), None),
            P(),
            P(),
            P(),
            P(),
            P(),
            P(),
        ),
        out_specs=(
            P("dp", "seq", None),
            P("dp", "seq", None),
            P(("seq", "dp"), None),
            P(("seq", "dp"), None),
            P(("seq", "dp"), None),
            P(("seq", "dp"), None),
            P(("seq", "dp"), None),
            P(("seq", "dp")),
            P(("seq", "dp")),
            P(("seq", "dp")),
            P(("seq", "dp")),
            P(("seq", "dp")),
            P(("seq", "dp")),
        ),
        check_vma=False,
    )
```

```python
import math

import functools

import jax
import jax.numpy as jnp
from jax import lax
from jax.experimental import pallas as pl
from jax.experimental.pallas import tpu as pltpu
from jax.sharding import PartitionSpec as P

HEADS = 4
HEAD_DIM = 256
WINDOW = 512


EPSILON = 1e-06
GELU_SLOPE = math.sqrt(2.0 / math.pi)
GELU_CUBIC = 0.044715


def bits_of(count):
    bits = []
    bit = 1
    while bit < count:
        bits.append(bit)
        bit *= 2
    return bits


def one_hot_order(origin, count):
    return (jnp.arange(count, dtype=jnp.int32)[:, None] == origin[None, :]).astype(jnp.bfloat16)


def in_order(value, order):
    high = value.astype(jnp.bfloat16)
    low = (value - high.astype(jnp.float32)).astype(jnp.bfloat16)
    return contract_cols(high, order) + contract_cols(low, order)


def inv_root(vector):
    return lax.rsqrt(jnp.mean(vector * vector, axis=-1, keepdims=True) + EPSILON)


def norm_back(grad, unit_part, root_part, gain):
    scaled = grad * gain
    return root_part * (scaled - unit_part * jnp.mean(scaled * unit_part, axis=-1, keepdims=True))


def gelu_pair(gate):
    inner = jnp.tanh(GELU_SLOPE * (gate + GELU_CUBIC * gate * gate * gate))
    gelu_value = 0.5 * gate * (1.0 + inner)
    gelu_slope = 0.5 * (1.0 + inner) + 0.5 * gate * (1.0 - inner * inner) * GELU_SLOPE * (
        1.0 + 3.0 * GELU_CUBIC * gate * gate
    )
    return (gelu_value, gelu_slope)


def turn_half(vector):
    half = vector.shape[-1] // 2
    return jnp.concatenate([-vector[..., half:], vector[..., :half]], axis=-1)


def seq_begin(index, starts):
    return jnp.max(jnp.where(starts[None, :] <= index[:, None], starts[None, :], 0), axis=1)


def rope_tables(position, head):
    freq = jnp.exp(-math.log(10000.0) * jnp.arange(head // 2, dtype=jnp.float32) * (2.0 / head))
    angle = position[:, None] * freq[None, :]
    angle = jnp.concatenate([angle, angle], axis=1)
    return (jnp.cos(angle), jnp.sin(angle))


def dot32(left, right):
    return jnp.dot(left, right, preferred_element_type=jnp.float32)


def contract_rows(left, right):
    return lax.dot_general(
        left, right, (((0,), (0,)), ((), ())), preferred_element_type=jnp.float32
    )


def contract_cols(left, right):
    return lax.dot_general(
        left, right, (((1,), (1,)), ((), ())), preferred_element_type=jnp.float32
    )


MESH = pl.DeviceIdType.MESH


def group_width(dp_count):
    return dp_count // 2


def flip(value, other, count):
    if count & (count - 1):
        return (value + other) % count
    total = 0
    for bit in bits_of(count):
        total = total + ((value // bit + other // bit) % 2) * bit
    return total


def column_tiles(width):
    best = 128
    for size in range(128, 513, 128):
        if width % size == 0:
            best = size
    return [slice(at, at + best) for at in range(0, width, best)]


def nt(left, right):
    return lax.dot_general(left, right, (((1,), (1,)), ((), ())), preferred_element_type=jnp.float32)


def tn(left, right):
    return lax.dot_general(left, right, (((0,), (0,)), ((), ())), preferred_element_type=jnp.float32)


def ffn_kernel(zs, ys, ws, rows, width, own, *refs):
    half = ws // 2
    x_ref, hidden_ref, grad_ref, gain_ref = refs[:4]
    w_refs = refs[4 : 4 + 3 * half]
    result_ref, gg_ref, in_grad_ref, kept_ref = refs[4 + 3 * half : 8 + 3 * half]
    at = 8 + 3 * half
    passed_ref = None
    if half > 1:
        passed_ref = refs[at]
        at += 1
    (tok, grd, wt, gate, up, hid, dgb, dub, acc, part, grad_own, ysend, yrecv, zsend, zrecv, dwsend, dwrecv) = refs[
        at : at + 17
    ]
    (agz_s, agy_s, ag_r, ry_s, ry_r, rz_s, rz_r, wl_s, wr_s, wr_r, dw_s, dw_r) = refs[at + 17 :]
    z = lax.axis_index("seq")
    d = lax.axis_index("dp")
    y = d // ws
    w = d % ws
    mate = y * ws + w + 1 - 2 * (w % 2)
    pair = ys * rows
    tiles = column_tiles(width)

    def peer(zz, yy):
        return (zz, yy * ws + w)

    def block(zz, yy):
        return pl.ds(pl.multiple_of((zz * ys + yy) * rows, rows), rows)

    def span(zz):
        return pl.ds(pl.multiple_of(zz * pair, pair), pair)

    barrier = pltpu.get_barrier_semaphore()
    for dz in range(1, zs):
        pl.semaphore_signal(barrier, inc=1, device_id=peer(flip(z, dz, zs), y), device_id_type=MESH)
    for dy in range(1, ys):
        pl.semaphore_signal(barrier, inc=1, device_id=peer(z, (y + dy) % ys), device_id_type=MESH)
    pl.semaphore_signal(barrier, inc=1, device_id=(z, mate), device_id_type=MESH)
    for i in range(half):
        for m in range(3):
            pltpu.make_async_copy(w_refs[3 * i + m], wt.at[m, 2 * i], wl_s.at[i, m]).start()
    pl.semaphore_wait(barrier, zs + ys - 1)

    def copy_z(p, src, buf, dz):
        return pltpu.make_async_remote_copy(
            src_ref=src,
            dst_ref=buf.at[block(z, y)],
            send_sem=agz_s.at[p, dz],
            recv_sem=ag_r.at[p, z, y],
            device_id=peer(flip(z, dz, zs), y),
            device_id_type=MESH,
        )

    def copy_y(p, src, buf, zz, dy):
        return pltpu.make_async_remote_copy(
            src_ref=src,
            dst_ref=buf.at[block(zz, y)],
            send_sem=agy_s.at[p, zz, dy],
            recv_sem=ag_r.at[p, zz, y],
            device_id=peer(z, (y + dy) % ys),
            device_id_type=MESH,
        )

    def arrived(p, buf, zz, yy):
        pltpu.make_async_remote_copy(
            src_ref=buf.at[block(zz, yy)],
            dst_ref=buf.at[block(zz, yy)],
            send_sem=agz_s.at[p, 0],
            recv_sem=ag_r.at[p, zz, yy],
            device_id=peer(z, y),
            device_id_type=MESH,
        ).wait_recv()

    def copy_wide(i, m):
        return pltpu.make_async_remote_copy(
            src_ref=w_refs[3 * i + m],
            dst_ref=wt.at[m, 2 * i + 1],
            send_sem=wr_s.at[i, m],
            recv_sem=wr_r.at[i, m],
            device_id=(z, mate),
            device_id_type=MESH,
        )

    def reduce_y(p, zz, dy):
        return pltpu.make_async_remote_copy(
            src_ref=ysend.at[dy - 1, zz],
            dst_ref=yrecv.at[ys - dy - 1, zz],
            send_sem=ry_s.at[p, dy - 1, zz],
            recv_sem=ry_r.at[p, ys - dy - 1, zz],
            device_id=peer(z, (y + dy) % ys),
            device_id_type=MESH,
        )

    def reduce_z(p, zz):
        return pltpu.make_async_remote_copy(
            src_ref=zsend.at[zz],
            dst_ref=zrecv.at[z],
            send_sem=rz_s.at[p, zz],
            recv_sem=rz_r.at[p, z],
            device_id=peer(zz, y),
            device_id_type=MESH,
        )

    def reduced(p, zz):
        return pltpu.make_async_remote_copy(
            src_ref=zsend.at[zz],
            dst_ref=zrecv.at[zz],
            send_sem=rz_s.at[p, zz],
            recv_sem=rz_r.at[p, zz],
            device_id=peer(z, y),
            device_id_type=MESH,
        )

    def combine(p, zz, mine):
        total = part[zz]
        for dy in range(1, ys):
            reduce_y(p, zz, dy).wait_recv()
            total = total + yrecv[ys - dy - 1, zz].astype(jnp.float32)
        if mine:
            part[zz] = total
        else:
            zsend[zz] = total.astype(jnp.bfloat16)
            reduce_z(p, zz).start()

    def phase(p, src, buf, compute, ready, between):
        for dy in range(1, ys):
            copy_y(p, src, buf, z, dy).start()
        for dz in range(1, zs):
            copy_z(p, src, buf, dz).start()
        buf[block(z, y), :] = src[...]
        ready()

        def step(dz, carry):
            zz = flip(z, dz, zs)

            @pl.when(dz + 1 < zs)
            def _():
                nxt = flip(z, dz + 1, zs)
                arrived(p, buf, nxt, y)
                for dy in range(1, ys):
                    copy_y(p, buf.at[block(nxt, y)], buf, nxt, dy).start()

            for dy in range(1, ys):
                arrived(p, buf, zz, (y + dy) % ys)
            compute(zz)
            for dy in range(1, ys):
                yy = (y + dy) % ys
                ysend[dy - 1, zz] = acc[pl.ds(pl.multiple_of(yy * rows, rows), rows), :].astype(jnp.bfloat16)
                reduce_y(p, zz, dy).start()
            part[zz] = acc[pl.ds(pl.multiple_of(y * rows, rows), rows), :]

            @pl.when(dz == 1)
            def _():
                combine(p, z, True)

            @pl.when(dz > 1)
            def _():
                combine(p, flip(z, dz - 1, zs), False)

            return carry

        lax.fori_loop(0, zs, step, 0)
        combine(p, flip(z, zs - 1, zs), zs == 1)
        between()
        total = part[z]
        for dz in range(1, zs):
            zz = flip(z, dz, zs)
            reduced(p, zz).wait_recv()
            total = total + zrecv[zz].astype(jnp.float32)
        return total

    def sent(p, src, buf):
        for dz in range(1, zs):
            copy_z(p, src, buf, dz).wait_send()
            reduce_z(p, flip(z, dz, zs)).wait_send()
        for zz in range(zs):
            for dy in range(1, ys):
                copy_y(p, src, buf, zz, dy).wait_send()
                reduce_y(p, zz, dy).wait_send()

    def forward(zz):
        acc[...] = jnp.zeros_like(acc)

        def shard(s, carry):
            x = tok[span(zz), :]
            gate_part = nt(x, wt[0, s])
            up_part = nt(x, wt[1, s])
            gate[s, span(zz), :] = gate_part
            up[s, span(zz), :] = up_part
            inner = jnp.tanh(GELU_SLOPE * (gate_part + GELU_CUBIC * gate_part * gate_part * gate_part))
            hidden = (0.5 * gate_part * (1.0 + inner) * up_part).astype(jnp.bfloat16)
            hid[s, span(zz), :] = hidden
            for tile in tiles:
                acc[:, tile] = acc[:, tile] + dot32(hidden, wt[2, s, :, tile])
            return carry

        lax.fori_loop(0, ws, shard, 0)

    def backward(zz):
        acc[...] = jnp.zeros_like(acc)

        def shard(s, carry):
            hidden_grad = nt(grd[span(zz), :], wt[2, s])
            gelu_value, gelu_slope = gelu_pair(gate[s, span(zz), :])
            dgate = (hidden_grad * up[s, span(zz), :] * gelu_slope).astype(jnp.bfloat16)
            dup = (hidden_grad * gelu_value).astype(jnp.bfloat16)
            dgb[s, span(zz), :] = dgate
            dub[s, span(zz), :] = dup
            for tile in tiles:
                acc[:, tile] = acc[:, tile] + dot32(dgate, wt[0, s, :, tile]) + dot32(dup, wt[1, s, :, tile])
            return carry

        lax.fori_loop(0, ws, shard, 0)

    def weights_ready():
        for i in range(half):
            for m in range(3):
                pltpu.make_async_copy(w_refs[3 * i + m], wt.at[m, 2 * i], wl_s.at[i, m]).wait()
        for i in range(half):
            for m in range(3):
                copy_wide(i, m).wait_recv()

    def nothing():
        return None

    def copy_dw(i, m):
        return pltpu.make_async_remote_copy(
            src_ref=dwsend.at[i, m],
            dst_ref=dwrecv.at[i, m],
            send_sem=dw_s.at[i, m],
            recv_sem=dw_r.at[i, m],
            device_id=(z, mate),
            device_id_type=MESH,
        )

    terms = ((dgb, tok), (dub, tok), (hid, grd))

    def weight_terms():
        for m in range(3):
            left, right = terms[m]

            def away(i, carry):
                for tile in tiles:
                    dwsend[i, m, :, tile] = tn(left[2 * i + 1], right[:, tile]).astype(jnp.bfloat16)
                copy_dw(i, m).start()
                return carry

            lax.fori_loop(0, half, away, 0)
        for m in range(3):
            left, right = terms[m]

            def home(i, carry):
                copy_dw(i, m).wait_recv()
                for tile in tiles:
                    total = tn(left[2 * i], right[:, tile]) + dwrecv[i, m, :, tile].astype(jnp.float32)

                    @pl.when(i == 0)
                    def _():
                        kept_ref[m, :, tile] = total

                    if half > 1:

                        @pl.when(i > 0)
                        def _():
                            passed_ref[jnp.maximum(i - 1, 0), m, :, tile] = total.astype(jnp.bfloat16)

                return carry

            lax.fori_loop(0, half, home, 0)

    for i in range(half):
        for m in range(3):
            copy_wide(i, m).start()
    ffn_out = phase(0, x_ref, tok, forward, weights_ready, nothing)
    root = inv_root(ffn_out)
    unit = ffn_out * root
    gain = gain_ref[...]
    result_ref[...] = hidden_ref[...] + unit * gain
    rows_grad = grad_ref[...]
    gg_ref[...] = jnp.sum(rows_grad * unit, axis=0, keepdims=True)
    grad_own[...] = norm_back(rows_grad, unit, root, gain).astype(jnp.bfloat16)
    sent(0, x_ref, tok)
    in_grad_ref[...] = phase(1, grad_own, grd, backward, nothing, weight_terms)

    for i in range(half):
        for m in range(3):
            copy_wide(i, m).wait_send()
            copy_dw(i, m).wait_send()
    sent(1, grad_own, grd)


def ffn_block(ffn_input, hidden_in, rows_grad, gain, ffn_rows, zs, dp_count):
    rows, width = ffn_input.shape
    own = ffn_rows[0][0].shape[0]
    ws = group_width(dp_count)
    ys = dp_count // ws
    half = ws // 2
    tokens = zs * ys * rows
    bf, f32 = jnp.bfloat16, jnp.float32
    vmem = pl.BlockSpec(memory_space=pltpu.VMEM)
    outs = [
        jax.ShapeDtypeStruct((rows, width), f32),
        jax.ShapeDtypeStruct((1, width), f32),
        jax.ShapeDtypeStruct((rows, width), f32),
        jax.ShapeDtypeStruct((3, own, width), f32),
    ]
    if half > 1:
        outs.append(jax.ShapeDtypeStruct((half - 1, 3, own, width), bf))
    dma = pltpu.SemaphoreType.DMA
    scratch = [
        pltpu.VMEM((tokens, width), bf),
        pltpu.VMEM((tokens, width), bf),
        pltpu.VMEM((3, ws, own, width), bf),
        pltpu.VMEM((ws, tokens, own), f32),
        pltpu.VMEM((ws, tokens, own), f32),
        pltpu.VMEM((ws, tokens, own), bf),
        pltpu.VMEM((ws, tokens, own), bf),
        pltpu.VMEM((ws, tokens, own), bf),
        pltpu.VMEM((ys * rows, width), f32),
        pltpu.VMEM((zs, rows, width), f32),
        pltpu.VMEM((rows, width), bf),
        pltpu.VMEM((ys - 1, zs, rows, width), bf),
        pltpu.VMEM((ys - 1, zs, rows, width), bf),
        pltpu.VMEM((zs, rows, width), bf),
        pltpu.VMEM((zs, rows, width), bf),
        pltpu.VMEM((half, 3, own, width), bf),
        pltpu.VMEM((half, 3, own, width), bf),
        dma((2, zs)),
        dma((2, zs, ys)),
        dma((2, zs, ys)),
        dma((2, ys - 1, zs)),
        dma((2, ys - 1, zs)),
        dma((2, zs)),
        dma((2, zs)),
        dma((half, 3)),
        dma((half, 3)),
        dma((half, 3)),
        dma((half, 3)),
        dma((half, 3)),
    ]
    flat = [w for group in ffn_rows for w in group]
    flops = 2 * tokens * ws * own * width * 9
    out = pl.pallas_call(
        functools.partial(ffn_kernel, zs, ys, ws, rows, width, own),
        out_shape=outs,
        in_specs=[vmem] * 4 + [pl.BlockSpec(memory_space=pl.ANY)] * len(flat),
        out_specs=[vmem] * len(outs),
        scratch_shapes=scratch,
        compiler_params=pltpu.CompilerParams(
            collective_id=1, has_side_effects=True, vmem_limit_bytes=67043328
        ),
        cost_estimate=pl.CostEstimate(flops=flops, bytes_accessed=40 << 20, transcendentals=0),
        name="ffn_block",
    )(ffn_input, hidden_in, rows_grad, gain[None, :], *flat)
    passed = out[4] if half > 1 else None
    return out[0], out[1], out[2], out[3], passed


def neighbours(zs, ys, xs):
    z = lax.axis_index("seq")
    d = lax.axis_index("dp")
    y, x, c = d // (2 * xs), (d // 2) % xs, d % 2

    def dev(zz, yy, xx, cc):
        return (zz, (yy * xs + xx) * 2 + cc)

    barrier = pltpu.get_barrier_semaphore()
    near = [dev(flip(z, dz, zs), y, x, c) for dz in range(1, zs)]
    near += [dev(z, (y + dy) % ys, x, c) for dy in range(1, ys)]
    near += [dev(z, y, flip(x, dx, xs), c) for dx in range(1, xs)]
    near += [dev(z, y, x, 1 - c)]
    for peer in near:
        pl.semaphore_signal(barrier, inc=1, device_id=peer, device_id_type=MESH)
    pl.semaphore_wait(barrier, len(near))
    return z, y, x, c, dev


def remote(src, dst, send, recv, to):
    return pltpu.make_async_remote_copy(
        src_ref=src, dst_ref=dst, send_sem=send, recv_sem=recv, device_id=to, device_id_type=MESH
    )


def spread_kernel(zs, ys, xs, with_kv, extras, *refs):
    refs = list(refs)
    w_ref = refs.pop(0)
    kv_ref = refs.pop(0) if with_kv else None
    extra_in = [refs.pop(0) for _ in range(extras)]
    out_ref = refs.pop(0)
    kv_out = refs.pop(0) if with_kv else None
    extra_out = [refs.pop(0) for _ in range(extras)]
    own_s, x_s, z_s, y_s, c_s, r, e_s, e_r = refs[:8]
    kv_own, kv_s, kv_r = refs[8:11] if with_kv else (None, None, None)
    z, y, x, c, dev = neighbours(zs, ys, xs)

    def slot(zz, yy, xx, cc):
        return out_ref.at[zz, yy, xx, cc]

    def copy(src, zz, yy, xx, send, to):
        return remote(src, slot(zz, yy, xx, c), send, r.at[zz, yy, xx, c], to)

    def over_x(dx):
        return copy(w_ref, z, y, x, x_s.at[dx], dev(z, y, flip(x, dx, xs), c))

    def over_z(src, dx, dz):
        return copy(src, z, y, flip(x, dx, xs), z_s.at[dx, dz], dev(flip(z, dz, zs), y, x, c))

    def over_y(src, zz, dx, dy):
        return copy(src, zz, y, flip(x, dx, xs), y_s.at[zz, dx, dy], dev(z, (y + dy) % ys, x, c))

    def over_core(src, zz, yy, xx):
        return copy(src, zz, yy, xx, c_s.at[zz, yy, xx], dev(z, y, x, 1 - c))

    def arrived(zz, yy, xx, cc):
        remote(slot(zz, yy, xx, cc), slot(zz, yy, xx, cc), x_s.at[0], r.at[zz, yy, xx, cc], dev(z, y, x, 1 - c)).wait_recv()

    def extra(e, dx):
        return remote(
            extra_in[e], extra_out[e].at[dx - 1], e_s.at[e, dx], e_r.at[e, dx], dev(z, y, flip(x, dx, xs), c)
        )

    def kv_copy(dz):
        return remote(kv_ref, kv_out.at[z], kv_s.at[dz], kv_r.at[z], dev(flip(z, dz, zs), y, x, c))

    def kv_arrived(zz):
        remote(kv_ref, kv_out.at[zz], kv_s.at[0], kv_r.at[zz], dev(z, y, x, 1 - c)).wait_recv()

    for dx in range(1, xs):
        over_x(dx).start()
    if with_kv:
        for dz in range(1, zs):
            kv_copy(dz).start()
    for dz in range(1, zs):
        over_z(w_ref, 0, dz).start()
    for dy in range(1, ys):
        over_y(w_ref, z, 0, dy).start()
    over_core(w_ref, z, y, x).start()
    for e in range(extras):
        for dx in range(1, xs):
            extra(e, dx).start()
    keep = pltpu.make_async_copy(w_ref, out_ref.at[z, y, x, c], own_s.at[0])
    keep.start()
    if with_kv:
        kv_keep = pltpu.make_async_copy(kv_ref, kv_out.at[z], kv_own.at[0])
        kv_keep.start()
    for dx in range(1, xs):
        xx = flip(x, dx, xs)
        arrived(z, y, xx, c)
        src = slot(z, y, xx, c)
        for dz in range(1, zs):
            over_z(src, dx, dz).start()
        for dy in range(1, ys):
            over_y(src, z, dx, dy).start()
        over_core(src, z, y, xx).start()

    def step(t, carry):
        @pl.when(t < zs)
        def _():
            zz = flip(z, t, zs)
            for dx in range(xs):
                xx = flip(x, dx, xs)
                arrived(zz, y, xx, c)
                src = slot(zz, y, xx, c)
                for dy in range(1, ys):
                    over_y(src, zz, dx, dy).start()
                over_core(src, zz, y, xx).start()

        zz = flip(z, t - 1, zs)
        for dx in range(xs):
            xx = flip(x, dx, xs)
            for dy in range(1, ys):
                yy = (y + dy) % ys
                arrived(zz, yy, xx, c)
                over_core(slot(zz, yy, xx, c), zz, yy, xx).start()
        return carry

    lax.fori_loop(1, zs + 1, step, 0)

    def settle(zz, carry):
        for yy in range(ys):
            for xx in range(xs):
                arrived(zz, yy, xx, 1 - c)
                over_core(slot(zz, yy, xx, c), zz, yy, xx).wait_send()
        for dx in range(xs):
            for dy in range(1, ys):
                over_y(slot(zz, y, x, c), zz, dx, dy).wait_send()
        return carry

    lax.fori_loop(0, zs, settle, 0)
    keep.wait()
    for dx in range(1, xs):
        over_x(dx).wait_send()
    for dz in range(1, zs):
        for dx in range(xs):
            over_z(w_ref, dx, dz).wait_send()
    if with_kv:
        kv_keep.wait()
        for dz in range(1, zs):
            kv_arrived(flip(z, dz, zs))
            kv_copy(dz).wait_send()
    for e in range(extras):
        for dx in range(1, xs):
            extra(e, dx).wait()


def spread(block, kv, extra, zs, dp_count, ident):
    own, width = block.shape
    ys, xs = 2, dp_count // 4
    bf = jnp.bfloat16
    dma = pltpu.SemaphoreType.DMA
    vmem, hbm = pl.BlockSpec(memory_space=pltpu.VMEM), pl.BlockSpec(memory_space=pl.ANY)
    outs = [jax.ShapeDtypeStruct((zs, ys, xs, 2, own, width), bf)]
    scratch = [dma((1,)), dma((xs,)), dma((xs, zs)), dma((zs, xs, ys)), dma((zs, ys, xs)), dma((zs, ys, xs, 2))]
    scratch += [dma((len(extra), xs))] * 2
    args, specs = [block], [vmem]
    if kv is not None:
        args.append(kv)
        specs.append(vmem)
        outs.append(jax.ShapeDtypeStruct((zs,) + kv.shape, bf))
        scratch += [dma((1,)), dma((zs,)), dma((zs,))]
    for e in extra:
        args.append(e)
        specs.append(hbm)
        outs.append(jax.ShapeDtypeStruct((xs - 1,) + e.shape, bf))
    out = pl.pallas_call(
        functools.partial(spread_kernel, zs, ys, xs, kv is not None, len(extra)),
        out_shape=outs,
        in_specs=specs,
        out_specs=[hbm] * len(outs),
        scratch_shapes=scratch,
        compiler_params=pltpu.CompilerParams(collective_id=ident, has_side_effects=True),
        cost_estimate=pl.CostEstimate(flops=1 << 20, bytes_accessed=24 << 20, transcendentals=0),
        name="spread",
    )(*args)
    return out[0].reshape(-1, own, width), (out[1] if kv is not None else None), out[len(out) - len(extra) :]


def fold_kernel(zs, ys, xs, with_kv, parts, *refs):
    refs = list(refs)
    term = refs.pop(0)
    kv_ref = refs.pop(0) if with_kv else None
    passed = refs.pop(0) if parts else None
    out_ref = refs.pop(0)
    kv_out = refs.pop(0) if with_kv else None
    got = refs.pop(0) if parts else None
    (crecv, s1, r2, s2, r3, s3, r4, c_s, c_r, y_s, y_r, z_s, z_r, x_s, x_r) = refs[:15]
    refs = refs[15:]
    e_s, e_r = (refs.pop(0), refs.pop(0)) if parts else (None, None)
    kv_got, kv_s, kv_r = refs if with_kv else (None, None, None)
    f32, bf = jnp.float32, jnp.bfloat16
    z, y, x, c, dev = neighbours(zs, ys, xs)

    def core_copy(zz, yy, xx):
        return remote(
            term.at[zz, yy, xx, 1 - c], crecv.at[zz, yy, xx], c_s.at[zz, yy, xx], c_r.at[zz, yy, xx], dev(z, y, x, 1 - c)
        )

    def kv_copy(dz):
        zz = flip(z, dz, zs)
        return remote(kv_ref.at[zz], kv_got.at[dz], kv_s.at[dz], kv_r.at[dz], dev(zz, y, x, c))

    def over_y(zz, xx, dy):
        yy = (y + dy) % ys
        at = ys - dy - 1
        return remote(
            s1.at[zz, yy, xx], r2.at[at, zz, xx], y_s.at[dy - 1, zz, xx], y_r.at[at, zz, xx], dev(z, yy, x, c)
        )

    def over_z(dz, xx):
        return remote(
            s2.at[dz, xx], r3.at[dz, xx], z_s.at[dz, xx], z_r.at[dz, xx], dev(flip(z, dz, zs), y, x, c)
        )

    def over_x(dx):
        return remote(s3.at[dx], r4.at[dx], x_s.at[dx], x_r.at[dx], dev(z, y, flip(x, dx, xs), c))

    def extra(k, dx):
        return remote(
            passed.at[dx - 1, parts[k]], got.at[dx - 1, k], e_s.at[k, dx], e_r.at[k, dx], dev(z, y, flip(x, dx, xs), c)
        )

    if with_kv:
        for dz in range(1, zs):
            kv_copy(dz).start()

    def first(t, carry):
        zz = flip(z, zs - 1 - t, zs)
        for yy in range(ys):
            for xx in range(xs):
                core_copy(zz, yy, xx).start()
        return carry

    lax.fori_loop(0, zs, first, 0)
    for k in range(len(parts)):
        for dx in range(1, xs):
            extra(k, dx).start()

    def step(t, carry):
        @pl.when(t < zs)
        def _():
            zz = flip(z, zs - 1 - t, zs)
            for dy in range(ys - 1, -1, -1):
                yy = (y + dy) % ys
                for xx in range(xs):
                    core_copy(zz, yy, xx).wait_recv()
                    total = term[zz, yy, xx, c].astype(f32) + crecv[zz, yy, xx].astype(f32)
                    s1[zz, yy, xx] = total.astype(bf)
                    if dy > 0:
                        over_y(zz, xx, dy).start()

        @pl.when(t >= 1)
        def _():
            dz = zs - t
            zz = flip(z, dz, zs)
            for xx in range(xs):
                total = s1[zz, y, xx].astype(f32)
                for dy in range(1, ys):
                    over_y(zz, xx, dy).wait_recv()
                    total = total + r2[ys - dy - 1, zz, xx].astype(f32)
                s2[dz, xx] = total.astype(bf)

                @pl.when(dz > 0)
                def _():
                    over_z(dz, xx).start()

        return carry

    lax.fori_loop(0, zs + 1, step, 0)
    for dx in range(xs - 1, -1, -1):
        xx = flip(x, dx, xs)
        total = s2[0, xx].astype(f32)
        for dz in range(1, zs):
            over_z(dz, xx).wait_recv()
            total = total + r3[dz, xx].astype(f32)
        if dx > 0:
            s3[dx] = total.astype(bf)
            over_x(dx).start()
    if with_kv:
        kv_total = kv_ref[z].astype(f32)
        for dz in range(1, zs):
            kv_copy(dz).wait_recv()
            kv_total = kv_total + kv_got[dz].astype(f32)
        kv_out[...] = kv_total
        for dz in range(1, zs):
            kv_copy(dz).wait_send()
    for dx in range(1, xs):
        over_x(dx).wait()
        total = total + r4[dx].astype(f32)
    out_ref[...] = total

    def settle(zz, carry):
        for yy in range(ys):
            for xx in range(xs):
                core_copy(zz, yy, xx).wait_send()
        for dy in range(1, ys):
            for xx in range(xs):
                over_y(zz, xx, dy).wait_send()
        return carry

    lax.fori_loop(0, zs, settle, 0)
    for dz in range(1, zs):
        for xx in range(xs):
            over_z(dz, xx).wait_send()
    for k in range(len(parts)):
        for dx in range(1, xs):
            extra(k, dx).wait()


def fold(term, kv, passed, parts, zs, dp_count, ident):
    own, width = term.shape[1:]
    ys, xs = 2, dp_count // 4
    bf, f32 = jnp.bfloat16, jnp.float32
    dma = pltpu.SemaphoreType.DMA
    vmem, hbm = pl.BlockSpec(memory_space=pltpu.VMEM), pl.BlockSpec(memory_space=pl.ANY)
    outs, out_specs = [jax.ShapeDtypeStruct((own, width), f32)], [vmem]
    args, specs = [term.reshape(zs, ys, xs, 2, own, width)], [vmem]
    lead = [(zs, ys, xs), (zs, ys, xs), (ys - 1, zs, xs), (zs, xs), (zs, xs), (xs,), (xs,)]
    scratch = [pltpu.VMEM(size + (own, width), bf) for size in lead]
    scratch += [dma((zs, ys, xs))] * 2 + [dma((ys - 1, zs, xs))] * 2 + [dma((zs, xs))] * 2 + [dma((xs,))] * 2
    if kv is not None:
        args.append(kv)
        specs.append(vmem)
        outs.append(jax.ShapeDtypeStruct(kv.shape[1:], f32))
        out_specs.append(vmem)
    if xs < 2:
        parts = ()
    if parts:
        args.append(passed)
        specs.append(hbm)
        outs.append(jax.ShapeDtypeStruct((xs - 1, len(parts)) + passed.shape[2:], bf))
        out_specs.append(hbm)
        scratch += [dma((len(parts), xs))] * 2
    if kv is not None:
        scratch += [pltpu.VMEM(kv.shape, bf), dma((zs,)), dma((zs,))]
    out = pl.pallas_call(
        functools.partial(fold_kernel, zs, ys, xs, kv is not None, parts),
        out_shape=outs,
        in_specs=specs,
        out_specs=out_specs,
        scratch_shapes=scratch,
        compiler_params=pltpu.CompilerParams(collective_id=ident, has_side_effects=True),
        cost_estimate=pl.CostEstimate(flops=1 << 20, bytes_accessed=24 << 20, transcendentals=0),
        name="fold",
    )(*args)
    return out[0], (out[1] if kv is not None else None), (out[-1] if parts else None)


def local(
    stream,
    stream_grad,
    lengths,
    w_qkv,
    w_out,
    w_gate,
    w_up,
    w_down,
    g_attn_in,
    g_query,
    g_key,
    g_attn_out,
    g_ffn_in,
    g_ffn_out,
):
    rows_in = stream[0]
    rows_grad = stream_grad[0]
    lens = lengths[0]
    rows = rows_in.shape[0]
    width = rows_in.shape[1]
    qwidth = HEADS * HEAD_DIM
    seq_count = lax.axis_size("seq")
    dp_count = lax.axis_size("dp")
    count = seq_count * dp_count
    keys = seq_count * rows
    scale = 1.0 / math.sqrt(HEAD_DIM)
    block_id = lax.axis_index("seq")
    qkv_own = w_qkv.shape[0]
    qkv_pad = (qkv_own + 8) // 8 * 8
    lane = jnp.arange(qkv_pad, dtype=jnp.int32)[None, :]
    owner = jnp.arange(count, dtype=jnp.int32)[:, None]
    qkv_origin = jnp.where(lane < qkv_own, owner * qkv_own + lane, -1).reshape(-1)
    qkv_order = one_hot_order(qkv_origin, width)
    w_qkv_pad = jnp.pad(w_qkv, ((0, qkv_pad - qkv_own), (0, 0)))
    qkv_full, _, (gate_rows, up_rows) = spread(w_qkv_pad, None, [w_gate, w_up], seq_count, dp_count, 2)
    qkv_full = qkv_full.reshape(count * qkv_pad, -1)
    groups = group_width(dp_count)
    starts = jnp.cumsum(lens) - lens
    own_index = block_id * rows + jnp.arange(rows, dtype=jnp.int32)
    key_index = jnp.arange(keys, dtype=jnp.int32)
    own_begin = seq_begin(own_index, starts)
    key_begin = seq_begin(key_index, starts)
    mask = (
        (key_begin[None, :] == own_begin[:, None])
        & (key_index[None, :] <= own_index[:, None])
        & (own_index[:, None] - key_index[None, :] < WINDOW)
    )
    full_mask = mask[:, None, :]
    cos_t, sin_t = rope_tables((own_index - own_begin).astype(jnp.float32), HEAD_DIM)
    root_attn = inv_root(rows_in)
    unit_attn = rows_in * root_attn
    attn_input = (unit_attn * g_attn_in).astype(jnp.bfloat16)
    attn_slots = dot32(attn_input, qkv_order).astype(jnp.bfloat16)
    projected = dot32(attn_slots, qkv_full)
    query = projected[:, :qwidth].reshape(rows, HEADS, HEAD_DIM)
    key_raw = projected[:, qwidth : qwidth + HEAD_DIM]
    value_raw = projected[:, qwidth + HEAD_DIM :]
    root_query = inv_root(query)
    unit_query = query * root_query
    query_norm = unit_query * g_query
    root_key = inv_root(key_raw)
    unit_key = key_raw * root_key
    key_norm = unit_key * g_key
    query_rot = query_norm * cos_t[:, None, :] + turn_half(query_norm) * sin_t[:, None, :]
    key_rot = key_norm * cos_t + turn_half(key_norm) * sin_t
    query_b = query_rot.astype(jnp.bfloat16)
    kv_own = jnp.concatenate([key_rot.astype(jnp.bfloat16), value_raw.astype(jnp.bfloat16)], axis=1)
    out_full, kv_all, (down_rows,) = spread(w_out, kv_own, [w_down], seq_count, dp_count, 3)
    ffn_rows = [(w_gate, w_up, w_down)] + [
        (gate_rows[i], up_rows[i], down_rows[i]) for i in range(groups // 2 - 1)
    ]
    out_full = out_full.reshape(qwidth, width)
    kv_all = kv_all.reshape(keys, 2 * HEAD_DIM)
    keys_b = kv_all[:, :HEAD_DIM]
    values_b = kv_all[:, HEAD_DIM:]
    scores = jnp.einsum("rhd,kd->rhk", query_b, keys_b, preferred_element_type=jnp.float32) * scale
    logsum = jnp.log(jnp.sum(jnp.where(full_mask, jnp.exp(scores), 0.0), axis=-1))
    probs = jnp.where(full_mask, jnp.exp(scores - logsum[..., None]), 0.0)
    probs_b = probs.astype(jnp.bfloat16)
    mixed = jnp.einsum("rhk,kd->rhd", probs_b, values_b, preferred_element_type=jnp.float32)
    mixed_b = mixed.reshape(rows, qwidth).astype(jnp.bfloat16)
    attn_out = dot32(mixed_b, out_full)
    root_post = inv_root(attn_out)
    unit_post = attn_out * root_post
    hidden_in = rows_in + unit_post * g_attn_out
    root_ffn = inv_root(hidden_in)
    unit_ffn = hidden_in * root_ffn
    ffn_input = (unit_ffn * g_ffn_in).astype(jnp.bfloat16)

    result, grad_g_ffn_out, ffn_in_grad, kept, passed = ffn_block(
        ffn_input, hidden_in, rows_grad, g_ffn_out, ffn_rows, seq_count, dp_count
    )
    grad_g_ffn_out = grad_g_ffn_out[0]
    grad_g_ffn_in = jnp.sum(ffn_in_grad * unit_ffn, axis=0)
    hidden_grad_in = rows_grad + norm_back(ffn_in_grad, unit_ffn, root_ffn, g_ffn_in)
    grad_g_attn_out = jnp.sum(hidden_grad_in * unit_post, axis=0)
    attn_grad_b = norm_back(hidden_grad_in, unit_post, root_post, g_attn_out).astype(jnp.bfloat16)
    mixed_grad_b = contract_cols(attn_grad_b, out_full).astype(jnp.bfloat16)
    out_term = contract_rows(mixed_b, attn_grad_b).astype(jnp.bfloat16).reshape((count,) + w_out.shape)
    mixed_grad3 = mixed_grad_b.reshape(rows, HEADS, HEAD_DIM)
    delta = jnp.sum(
        mixed_grad3.astype(jnp.float32)
        * mixed_b.reshape(rows, HEADS, HEAD_DIM).astype(jnp.float32),
        axis=-1,
    )
    scores_again = (
        jnp.einsum("rhd,kd->rhk", query_b, keys_b, preferred_element_type=jnp.float32) * scale
    )
    probs_again = jnp.where(full_mask, jnp.exp(scores_again - logsum[..., None]), 0.0)
    probs_again_b = probs_again.astype(jnp.bfloat16)
    value_grad_all = jnp.einsum(
        "rhk,rhd->kd", probs_again_b, mixed_grad3, preferred_element_type=jnp.float32
    )
    prob_grad = jnp.einsum("rhd,kd->rhk", mixed_grad3, values_b, preferred_element_type=jnp.float32)
    score_grad_b = (probs_again * (prob_grad - delta[..., None])).astype(jnp.bfloat16)
    query_rot_grad = (
        jnp.einsum("rhk,kd->rhd", score_grad_b, keys_b, preferred_element_type=jnp.float32) * scale
    )
    key_grad_all = (
        jnp.einsum("rhk,rhd->kd", score_grad_b, query_b, preferred_element_type=jnp.float32) * scale
    )
    kv_grad_all = jnp.concatenate([key_grad_all, value_grad_all], axis=1)
    owned_out, kv_grad, got_early = fold(
        out_term, kv_grad_all.astype(jnp.bfloat16).reshape(seq_count, rows, -1), passed, (0, 1), seq_count, dp_count, 4
    )
    key_rot_grad = kv_grad[:, :HEAD_DIM]
    value_grad = kv_grad[:, HEAD_DIM:]
    query_norm_grad = query_rot_grad * cos_t[:, None, :] - turn_half(
        query_rot_grad * sin_t[:, None, :]
    )
    key_norm_grad = key_rot_grad * cos_t - turn_half(key_rot_grad * sin_t)
    grad_g_query = jnp.sum(query_norm_grad * unit_query, axis=(0, 1))
    grad_g_key = jnp.sum(key_norm_grad * unit_key, axis=0)
    query_grad = norm_back(query_norm_grad, unit_query, root_query, g_query)
    key_grad = norm_back(key_norm_grad, unit_key, root_key, g_key)
    qkv_grad_b = jnp.concatenate(
        [query_grad.reshape(rows, qwidth), key_grad, value_grad], axis=1
    ).astype(jnp.bfloat16)
    attn_in_grad = in_order(contract_cols(qkv_grad_b, qkv_full), qkv_order)
    grad_g_attn_in = jnp.sum(attn_in_grad * unit_attn, axis=0)
    input_grad = hidden_grad_in + norm_back(attn_in_grad, unit_attn, root_attn, g_attn_in)
    gains = [grad_g_attn_in, grad_g_attn_out, grad_g_ffn_in, grad_g_ffn_out, grad_g_query, grad_g_key]
    gain_terms = jnp.concatenate([g.reshape(count, -1) for g in gains], axis=1)
    qkv_term = contract_rows(attn_slots, qkv_grad_b).astype(jnp.bfloat16).reshape(count, qkv_pad, -1)
    gain_rows = jnp.pad(gain_terms, ((0, 0), (0, w_qkv.shape[1] - gain_terms.shape[1]))).astype(jnp.bfloat16)
    qkv_term = jnp.where(
        jnp.arange(qkv_pad, dtype=jnp.int32)[None, :, None] == qkv_own, gain_rows[:, None, :], qkv_term
    )
    owned_all, _, got_late = fold(qkv_term, None, passed, (2,), seq_count, dp_count, 5)
    grads_ffn = [kept[0], kept[1], kept[2]]
    for i in range(groups // 2 - 1):
        for m, piece in enumerate((got_early[i, 0], got_early[i, 1], got_late[i, 0])):
            grads_ffn[m] = grads_ffn[m] + piece.astype(jnp.float32)
    grad_w_gate, grad_w_up, grad_w_down = grads_ffn
    owned_qkv = owned_all[:qkv_own]
    owned = owned_all[qkv_own]
    own_width, own_head = width // count, HEAD_DIM // count
    owned_gains = [owned[i * own_width : (i + 1) * own_width] for i in range(4)]
    owned_heads = [
        owned[4 * own_width + i * own_head : 4 * own_width + (i + 1) * own_head] for i in range(2)
    ]
    return (
        result[None],
        input_grad[None],
        owned_qkv,
        owned_out,
        grad_w_gate,
        grad_w_up,
        grad_w_down,
        owned_gains[0],
        owned_heads[0],
        owned_heads[1],
        owned_gains[1],
        owned_gains[2],
        owned_gains[3],
    )


def solution(mesh):
    return jax.shard_map(
        local,
        mesh=mesh,
        in_specs=(
            P("dp", "seq", None),
            P("dp", "seq", None),
            P("dp", None),
            P(("seq", "dp"), None),
            P(("seq", "dp"), None),
            P(("seq", "dp"), None),
            P(("seq", "dp"), None),
            P(("seq", "dp"), None),
            P(),
            P(),
            P(),
            P(),
            P(),
            P(),
        ),
        out_specs=(
            P("dp", "seq", None),
            P("dp", "seq", None),
            P(("seq", "dp"), None),
            P(("seq", "dp"), None),
            P(("seq", "dp"), None),
            P(("seq", "dp"), None),
            P(("seq", "dp"), None),
            P(("seq", "dp")),
            P(("seq", "dp")),
            P(("seq", "dp")),
            P(("seq", "dp")),
            P(("seq", "dp")),
            P(("seq", "dp")),
        ),
        check_vma=False,
    )
```
